512 devices in a mesh: gx: 32 (over y, x, z_hi), gy: 8 (over z_lo), gz: 2 (over core).
Axes of the slice: x: 4, y: 4, z: 16 (z_hi: 2, z_lo: 8; z = z_hi * 8 + z_lo), core: 2. Of those that a mesh axis runs over, the one named last changes fastest.
Arguments:
- source: float32 [256, 64, 4096], P('gx', 'gz', 'gy'), may hold values from -24 to 24
- coef: float32 [256, 64, 128], P('gx', 'gz', 'gy'), may hold values from 0.01 to 0.05
- face_trace: int32 [256, 2, 128], P('gx', 'gz'), may hold values from 0 to 1023, as said below
- near_col: int32 [32, 2, 8], P('gx', 'gz', 'gy'), may hold values from 0 to 63, as said below
- far_col: int32 [32, 2, 8, 7], P('gx', 'gz', 'gy'), may hold values from 0 to 63, as said below
- near_tile: bfloat16 [32, 2, 8, 1024, 1024], P('gx', 'gz', 'gy'), may hold values from -0.1875 to 0.1875
- far_u: bfloat16 [32, 2, 8, 7, 16, 1024], P('gx', 'gz', 'gy'), may hold values from -0.1875 to 0.1875
- far_v: bfloat16 [32, 2, 8, 7, 16, 1024], P('gx', 'gz', 'gy'), may hold values from -0.1875 to 0.1875
Outputs:
- solution: float32 [256, 64, 4096], P('gx', 'gz', 'gy')
- flux: float32 [256, 2, 4096], P('gx', 'gz', 'gy')
The draws below stay inside these ranges and needn't reach their ends.
Inputs may be any that keep to these rules, and one draw needn't show every extreme that they name: For every block of 8 rows of x and each face s, the entries face_trace(x, s, y) of that block are a permutation of 0 to 1023. For every row block, near_col over the slots j together with far_col over j and k name each column block 0 to 63 exactly once. `far_col`: see near_col: near and far column blocks of a row block together name every column block exactly once.
All inputs are finite; a program needn't handle non-finite values.
Results may differ from the reference program's by a relative error of at most 0.003.
Values may be sent and summed in bfloat16 or wider, within the bound.
A program may use at most 64 MiB of HBM per device.

```python
import math
import jax
import jax.numpy as jnp
from jax import lax

E = 32
TILE = 1024
RANK = 16
SWEEPS = 3
CX = 8
NX = 256
NY = 128
NZ = 64
NBLK = 64
COLS = 8
FAR = 7
N_GX = 32
N_GY = 8


def column_lists(key):
    keys = jax.random.split(jax.random.fold_in(key, 17), NBLK)
    perms = jax.vmap(lambda k: jax.random.permutation(k, NBLK))(keys).astype(jnp.int32)
    return perms.reshape(NBLK // 2, 2, NBLK // COLS, COLS)


def draw_near_col(key, part):
    return column_lists(key)[..., 0]


def draw_far_col(key, part):
    return column_lists(key)[..., 1:]


def draw_face_trace(key, part):
    keys = jax.random.split(jax.random.fold_in(key, 29), NBLK)
    perms = jax.vmap(lambda k: jax.random.permutation(k, TILE))(keys).astype(jnp.int32)
    return perms.reshape(NBLK // 2, 2, CX, NY).transpose(0, 2, 1, 3).reshape(NX, 2, NY)


def draw_source(key, part):
    subkeys = jax.random.split(jax.random.fold_in(key, 41), 2)
    x_index = jnp.arange(NX, dtype=jnp.int32)[:, None, None, None]
    z_index = jnp.arange(NZ, dtype=jnp.int32)[None, :, None, None]
    y_index = jnp.arange(NY, dtype=jnp.int32)[None, None, :, None]
    parity = (1 - 2 * ((x_index + y_index + z_index) % 2)).astype(jnp.float32)
    envelope = jnp.sin(math.pi * (x_index.astype(jnp.float32) + 0.5) / NX)
    envelope = envelope * jnp.sin(math.pi * (z_index.astype(jnp.float32) + 0.5) / NZ)
    envelope = envelope * jnp.sin(math.pi * (y_index.astype(jnp.float32) + 0.5) / NY)
    polarity = (1 - 2 * jax.random.randint(subkeys[0], (E,), 0, 2)).astype(jnp.float32)
    amplitude = 20.0
    jitter = 0.15 * jnp.clip(jax.random.normal(subkeys[1], (NX, NZ, NY, E), jnp.float32), -3.0, 3.0)
    drawn = amplitude * envelope * parity * polarity + jitter
    return drawn.reshape(NX, NZ, NY * E).astype(jnp.float32)


def steps_of(key, extent, shards, smallest, top_value):
    factor_of = 1.0
    for dim, blocks in shards:
        draws = jax.random.uniform(jax.random.fold_in(jax.random.fold_in(key, 6), dim), (blocks,), jnp.float32, smallest / len(shards), top_value / len(shards))
        factor_of = factor_of * jnp.repeat(jnp.exp(draws), extent[dim] // blocks).reshape((-1,) + (1,) * (len(extent) - 1 - dim))
    return factor_of


def gaussian(own_key, shape, scale, limit, shards=(), held_as=jnp.bfloat16):
    values = jax.random.normal(own_key, shape, jnp.float32) * scale
    if len(shards) > 0:
        values = steps_of(own_key, shape, shards, -0.22, 0.18) * values
    return jnp.clip(values, min=-limit, max=limit).astype(held_as)


def setup_inputs(seed: int = 0) -> dict:
    seeds = jax.random.split(jax.random.key(seed), 9)
    source = draw_source(jax.random.fold_in(seeds[8], 71), 0)
    coef = jnp.clip(jnp.exp(math.log(0.05) - 1.609438 * jax.random.uniform(seeds[1], (NX, NZ, NY), jnp.float32) ** steps_of(seeds[1], (NX, NZ, NY), ((0, 32), (1, 2), (2, 8)), -0.2, 0.2)), 0.01, 0.05)
    face_trace = draw_face_trace(jax.random.fold_in(seeds[8], 71), 0)
    near_col = draw_near_col(jax.random.fold_in(seeds[8], 71), 0)
    far_col = draw_far_col(jax.random.fold_in(seeds[8], 71), 0)
    near_tile = gaussian(seeds[5], (N_GX, 2, N_GY, TILE, TILE), TILE ** -0.5, 0.1875, ((0, 32), (1, 2), (2, 8)))
    far_u = gaussian(seeds[6], (N_GX, 2, N_GY, FAR, RANK, TILE), (RANK * NBLK) ** -0.5, 0.1875, ((0, 32), (1, 2), (2, 8)))
    far_v = gaussian(seeds[7], (N_GX, 2, N_GY, FAR, RANK, TILE), TILE ** -0.5, 0.1875, ((0, 32), (1, 2), (2, 8)))
    return {"source": source, "coef": coef, "face_trace": face_trace, "near_col": near_col, "far_col": far_col, "near_tile": near_tile, "far_u": far_u, "far_v": far_v}


def sweep(field, rhs, diag):
    padded = jnp.pad(field, ((1, 1), (1, 1), (0, 0)))
    zeros_rim = jnp.zeros((field.shape[0], field.shape[1], E), field.dtype)
    yplus = jnp.concatenate([field[:, :, E:], zeros_rim], axis=2)
    yminus = jnp.concatenate([zeros_rim, field[:, :, :-E]], axis=2)
    beside = padded[2:, 1:-1] + padded[:-2, 1:-1] + padded[1:-1, 2:] + padded[1:-1, :-2]
    beside = beside + yplus + yminus
    return (rhs + beside) / diag


def reference(source, coef, face_trace, near_col, far_col, near_tile, far_u, far_v):
    diag = jnp.repeat(6.0 + coef, E, axis=2)
    field = jnp.zeros(source.shape, source.dtype)
    for step in range(SWEEPS):
        field = sweep(field, source, diag)
    facevalue = jnp.stack([field[:, 0, :], field[:, NZ - 1, :]], axis=1).astype(jnp.bfloat16)
    blocks = facevalue.reshape(NBLK // 2, CX, 2, NY, E).transpose(0, 2, 1, 3, 4).reshape(NBLK, TILE, E)
    perms = face_trace.reshape(NBLK // 2, CX, 2, NY).transpose(0, 2, 1, 3).reshape(NBLK, TILE).astype(jnp.int32)
    rowids = jnp.arange(NBLK, dtype=jnp.int32)[:, None]
    traces = jnp.zeros((NBLK, TILE, E), jnp.bfloat16).at[rowids, perms].set(blocks)

    near_all = near_tile.reshape(NBLK, N_GY, TILE, TILE)
    u_all = far_u.reshape(NBLK, N_GY, FAR, RANK, TILE)
    v_all = far_v.reshape(NBLK, N_GY, FAR, RANK, TILE)
    ncol_all = near_col.reshape(NBLK, N_GY).astype(jnp.int32)
    fcol_all = far_col.reshape(NBLK, N_GY, FAR).astype(jnp.int32)

    def one_row(items):
        tiles, ufac, vfac, ncol, fcol = items
        near_traces = traces[ncol]
        nearpart = jnp.einsum('gij,gje->ie', tiles.astype(jnp.float32), near_traces.astype(jnp.float32))
        far_traces = traces[fcol]
        weights = jnp.einsum('gfrt,gfte->gfre', vfac.astype(jnp.float32), far_traces.astype(jnp.float32)).astype(jnp.bfloat16)
        farpart = jnp.einsum('gfrt,gfre->te', ufac.astype(jnp.float32), weights.astype(jnp.float32))
        return nearpart + farpart

    rows = lax.map(one_row, (near_all, u_all, v_all, ncol_all, fcol_all))
    picked = jnp.take_along_axis(rows, perms[:, :, None], axis=1)
    flux = picked.reshape(NBLK // 2, 2, CX, NY, E).transpose(0, 2, 1, 3, 4).reshape(NX, 2, NY * E)
    rhs = source.at[:, 0, :].add(flux[:, 0, :]).at[:, NZ - 1, :].add(flux[:, 1, :])
    solution = sweep(field, rhs, diag)
    return solution, flux
```

```python
import functools

import jax
import jax.numpy as jnp
from jax import lax
from jax.experimental import pallas as pl
from jax.experimental.pallas import tpu as pltpu
from jax.sharding import PartitionSpec as P

E = 32
CX = 8
YC = 16
DZ = 32
W = YC * E
L = 128
F32 = jnp.float32
BF16 = jnp.bfloat16
I32 = jnp.int32
MESH = pl.DeviceIdType.MESH
HIGHEST = lax.Precision.HIGHEST


def dot_nt(a, b):
    return lax.dot_general(a, b, (((1,), (1,)), ((), ())), preferred_element_type=F32)


def dot_tn(a, b):
    return lax.dot_general(a, b, (((0,), (0,)), ((), ())), preferred_element_type=F32)


def dot_nn(a, b):
    return lax.dot_general(a, b, (((1,), (0,)), ((), ())), preferred_element_type=F32)


def iota(shape, dim):
    return lax.broadcasted_iota(I32, shape, dim)


def along_x(field, low, high):
    rows = iota(field.shape, 0)
    before = jnp.where(rows == 0, low, pltpu.roll(field, 1, 0))
    after = jnp.where(rows == field.shape[0] - 1, high, pltpu.roll(field, field.shape[0] - 1, 0))
    return before + after


def along_y(field, low, high):
    n = field.shape[0]
    lanes = iota((n, L), 1)
    before = pltpu.roll(field, E, 1)
    after = pltpu.roll(field, W - E, 1)
    first = jnp.where(lanes < E, low, before[:, :L])
    last = jnp.where(lanes >= L - E, high, after[:, W - L :])
    before = jnp.concatenate([first, before[:, L:]], axis=1)
    after = jnp.concatenate([after[:, : W - L], last], axis=1)
    return before + after


def kernel(
    cfg,
    ncol, fcol, src, coef, ft, near_h, u_h, v_h,
    sol, flux,
    u1, u2, u3, rinv, planes,
    xs, xr, ys, yr, cr,
    vys, vyr, vzs, vzr,
    ftr, cols_v, cols_s,
    pick, mask, faces, gath,
    near_v, near_p, onehot, u_v, u_p,
    vparts, vblk, tsel, ns, nr, ws, wr, rs, rr,
    load_sem, x_ss, x_rs, c_ss, c_rs, v_ss, v_rs, ft_sem, col_ss, col_rs, smem_sem,
    f_ss, f_rs, g_ss, g_rs, k_ss, k_rs, vp_ss, vp_rs, n_ss, n_rs, w_ss, w_rs, r_ss, r_rs,
):
    n_gx, n_gy, far, rank, total_y = cfg
    tile = CX * total_y
    nq = n_gx // 2
    ring = 2 * n_gy
    gx = lax.axis_index("gx")
    gy = lax.axis_index("gy")
    gz = lax.axis_index("gz")
    zh = lax.rem(gx, 2)
    q = lax.div(gx, 2)
    anti = gx + 1 - 2 * zh
    other = 1 - gz
    me = zh * n_gy + gy
    low_x, high_x = gx > 0, gx < n_gx - 1
    low_y, high_y = gy > 0, gy < n_gy - 1

    def remote(a, b, ssem, rsem, dev):
        return pltpu.make_async_remote_copy(
            src_ref=a, dst_ref=b, send_sem=ssem, recv_sem=rsem, device_id=dev, device_id_type=MESH
        )

    bar = pltpu.get_barrier_semaphore()

    def signal(x, y, z):
        pl.semaphore_signal(bar, inc=1, device_id=(x, y, z), device_id_type=MESH)

    count = ring - 1 + nq - 1 + 1
    for dx, hx in ((-1, low_x), (1, high_x)):
        for dy, hy in ((-1, low_y), (0, None), (1, high_y)):
            cond = hx if hy is None else jnp.logical_and(hx, hy)
            count = count + cond.astype(I32)

            @pl.when(cond)
            def _(dx=dx, dy=dy):
                signal(gx + dx, gy + dy, gz)

    def ring_pos(d):
        pos = lax.rem(me + d, ring)
        return lax.div(pos, n_gy), lax.rem(pos, n_gy)

    def ring_signal(d, c):
        bz, by = ring_pos(d)
        signal(2 * q + bz, by, gz)
        return c

    lax.fori_loop(1, ring, ring_signal, 0)

    def xy_signal(d, c):
        signal(2 * lax.rem(q + d, nq) + zh, gy, gz)
        return c

    lax.fori_loop(1, nq, xy_signal, 0)
    signal(gx, gy, other)

    near_load = pltpu.make_async_copy(near_h, near_v, load_sem.at[0])
    u_load = pltpu.make_async_copy(u_h, u_v, load_sem.at[1])
    v_load = pltpu.make_async_copy(
        v_h.at[:, :, pl.ds(pl.multiple_of(gy * L, L), L)], vparts.at[gy], load_sem.at[2]
    )
    near_load.start()
    u_load.start()
    v_load.start()

    spread = (iota((YC, W), 0) == lax.div(iota((YC, W), 1), E)).astype(F32)

    def first(x, c):
        wide = jnp.dot(coef[x], spread, precision=HIGHEST, preferred_element_type=F32)
        r = 1.0 / (6.0 + wide)
        rinv[x] = r
        u1[x + 1] = src[x] * r
        return c

    lax.fori_loop(0, CX, first, 0)

    rows8 = iota((CX, W), 0)

    def plane(ref, off, depth):
        out = jnp.zeros((CX, W), F32)
        for x in range(CX):
            row = jnp.where(
                gz == 0,
                ref[x + off, depth : depth + 1, :],
                ref[x + off, DZ - 1 - depth : DZ - depth, :],
            )
            out = jnp.where(rows8 == x, row, out)
        return out

    for n, (ref, off, depth) in enumerate(
        ((src, 0, 0), (rinv, 0, 0), (u1, 1, 1), (u1, 1, 0), (src, 0, 1), (rinv, 0, 1), (u1, 1, 2))
    ):
        planes[n] = plane(ref, off, depth)
    for side, (edge, inner, lane) in enumerate(((0, 1, 0), (CX - 1, CX - 2, W - L))):
        for n in range(3):
            xs[side, n : n + 1, :] = planes[n, edge : edge + 1, :]
        xs[side, 3:4, :] = planes[3, inner : inner + 1, :]
        for n in range(4):
            ys[side, n] = planes[n, :, lane : lane + L]

    lanes_col = iota((8, L), 1)
    row = jnp.where(lanes_col == 0, ncol[0], 0)
    for k in range(far):
        row = jnp.where(lanes_col == k + 1, fcol[k], row)
    cols_v[gy] = row

    lanes32 = lax.div(iota((DZ, L), 1), E)

    def pack(u, n):
        def step(k, c):
            low = jnp.zeros((DZ, L), F32)
            high = jnp.zeros((DZ, L), F32)
            for j in range(4):
                cell = u[4 * k + j + 1]
                low = jnp.where(lanes32 == j, pltpu.roll(cell[:, :L], E * j, 1), low)
                high = jnp.where(
                    lanes32 == j, pltpu.roll(cell[:, W - L :], (E * j - (L - E)) % L, 1), high
                )
            vys[n, 0, k] = low
            vys[n, 1, k] = high
            return c

        lax.fori_loop(0, CX // 4, step, 0)

        def zstep(x, c):
            vzs[n, x] = jnp.where(gz == 0, u[x + 1, DZ - 1 : DZ, :], u[x + 1, 0:1, :])
            return c

        lax.fori_loop(0, CX, zstep, 0)

    pack(u1, 0)

    for side, have in ((0, low_x), (1, high_x)):

        @pl.when(jnp.logical_not(have))
        def _(side=side):
            xr[side] = jnp.zeros((4, W), F32)
            for u in (u1, u2, u3):
                u[side * (CX + 1)] = jnp.zeros((DZ, W), F32)

    for side, have in ((0, low_y), (1, high_y)):

        @pl.when(jnp.logical_not(have))
        def _(side=side):
            yr[side] = jnp.zeros((4, CX, L), F32)
            for n in range(3):
                vyr[n, side] = jnp.zeros((CX // 4, DZ, L), F32)

    for a, hx in ((0, low_x), (1, high_x)):
        for b, hy in ((0, low_y), (1, high_y)):

            @pl.when(jnp.logical_not(jnp.logical_and(hx, hy)))
            def _(a=a, b=b):
                cr[2 * a + b] = jnp.zeros((CX, L), F32)

    pl.semaphore_wait(bar, count)

    sides = ((0, low_x, -1), (1, high_x, 1))
    sides_y = ((0, low_y, -1), (1, high_y, 1))

    def x_copy(side, dx):
        return remote(xs.at[side], xr.at[1 - side], x_ss.at[side], x_rs.at[1 - side], (gx + dx, gy, gz))

    def y_copy(side, dy):
        return remote(
            ys.at[side], yr.at[1 - side], x_ss.at[2 + side], x_rs.at[3 - side], (gx, gy + dy, gz)
        )

    def c_copy(a, dx, b, dy):
        there = 2 * (1 - a) + 1 - b
        return remote(
            ys.at[b, 3], cr.at[there], c_ss.at[2 * a + b], c_rs.at[there], (gx + dx, gy + dy, gz)
        )

    def x_halo(act):
        for side, have, dx in sides:

            @pl.when(have)
            def _(side=side, dx=dx):
                act(x_copy(side, dx), 0)

    def c_halo(act):
        for a, hx, dx in sides:
            for b, hy, dy in sides_y:

                @pl.when(jnp.logical_and(hx, hy))
                def _(a=a, dx=dx, b=b, dy=dy):
                    act(c_copy(a, dx, b, dy), 0)

    def y_halo(act):
        for side, have, dy in sides_y:

            @pl.when(have)
            def _(side=side, dy=dy):
                act(y_copy(side, dy), 0)

    def narrow_recv():
        for side, have, dx in sides:

            @pl.when(have)
            def _(side=side, dx=dx):
                remote(
                    xs.at[side], xr.at[side], x_ss.at[side], x_rs.at[side], (gx + dx, gy, gz)
                ).wait_recv()

        for side, have, dy in sides_y:

            @pl.when(have)
            def _(side=side, dy=dy):
                remote(
                    ys.at[side], yr.at[side], x_ss.at[2 + side], x_rs.at[2 + side], (gx, gy + dy, gz)
                ).wait_recv()

        for a, hx, dx in sides:
            for b, hy, dy in sides_y:

                @pl.when(jnp.logical_and(hx, hy))
                def _(a=a, dx=dx, b=b, dy=dy):
                    remote(
                        ys.at[b, 3], cr.at[2 * a + b], c_ss.at[2 * a + b], c_rs.at[2 * a + b],
                        (gx + dx, gy + dy, gz),
                    ).wait_recv()

    def start(copy, _):
        copy.start()

    def sent(copy, _):
        copy.wait_send()

    x_halo(start)
    c_halo(start)
    y_halo(start)

    def ft_copy():
        return remote(ft, ftr, ft_sem.at[0], ft_sem.at[1], (anti, gy, gz))

    ft_copy().start()

    def peer(d):
        return lax.rem(gy + d, n_gy)

    def source_of(d):
        return lax.rem(gy + n_gy - d, n_gy)

    def col_send(d):
        return remote(cols_v.at[gy], cols_v.at[gy], col_ss.at[d], col_rs.at[d], (gx, peer(d), gz))

    def col_recv(d):
        s = source_of(d)
        return remote(cols_v.at[s], cols_v.at[s], col_ss.at[d], col_rs.at[d], (gx, s, gz))

    def vp_send(d):
        t = peer(d)
        return remote(
            v_h.at[:, :, pl.ds(pl.multiple_of(t * L, L), L)], vparts.at[gy],
            vp_ss.at[d], vp_rs.at[d], (gx, t, gz),
        )

    def vp_recv(d):
        s = source_of(d)
        return remote(vparts.at[s], vparts.at[s], vp_ss.at[d], vp_rs.at[d], (gx, s, gz))

    def each(n, f):
        def step(d, c):
            f(d)
            return c

        lax.fori_loop(1, n, step, 0)

    each(n_gy, lambda d: col_send(d).start())

    fields = (u1, u2, u3)

    def vol_send(n, act):
        u = fields[n]
        for side, have, dx in sides:

            @pl.when(have)
            def _(side=side, dx=dx):
                act(
                    remote(
                        u.at[1 + side * (CX - 1)], u.at[(1 - side) * (CX + 1)],
                        v_ss.at[n, side], v_rs.at[n, 1 - side], (gx + dx, gy, gz),
                    ),
                    0,
                )

        for side, have, dy in sides_y:

            @pl.when(have)
            def _(side=side, dy=dy):
                act(
                    remote(
                        vys.at[n, side], vyr.at[n, 1 - side],
                        v_ss.at[n, 2 + side], v_rs.at[n, 3 - side], (gx, gy + dy, gz),
                    ),
                    0,
                )

        act(remote(vzs.at[n], vzr.at[n], v_ss.at[n, 4], v_rs.at[n, 4], (gx, gy, other)), 0)

    def vol_recv(n):
        u = fields[n]
        for side, have, dx in sides:

            @pl.when(have)
            def _(side=side, dx=dx):
                halo = u.at[side * (CX + 1)]
                remote(halo, halo, v_ss.at[n, side], v_rs.at[n, side], (gx + dx, gy, gz)).wait_recv()

        for side, have, dy in sides_y:

            @pl.when(have)
            def _(side=side, dy=dy):
                halo = vyr.at[n, side]
                remote(
                    halo, halo, v_ss.at[n, 2 + side], v_rs.at[n, 2 + side], (gx, gy + dy, gz)
                ).wait_recv()

        remote(vzr.at[n], vzr.at[n], v_ss.at[n, 4], v_rs.at[n, 4], (gx, gy, other)).wait_recv()

    vol_send(0, start)
    each(n_gy, lambda d: vp_send(d).start())

    def tables(table, slot):
        spot = iota((L, total_y), 0) + gy * L
        col = iota((L, total_y), 1)
        cell = jnp.zeros((L, total_y), I32)
        for x in range(CX):
            cell = jnp.where(table[x] == spot, col + x * total_y, cell)
        cell = jnp.sum(cell.astype(F32), axis=1, keepdims=True).astype(I32)
        x = lax.div(cell, total_y)
        y = cell - x * total_y
        y8 = lax.div(y, 8)
        pick[slot] = (iota((L, 16 * n_gy), 1) == y8 * 8 + x).astype(BF16)
        mask[slot] = (lax.div(iota((L, 256), 1), E) == y - y8 * 8).astype(BF16)

    tables(ft, 0)
    spots = iota((tile, L), 0)
    for j in range(n_gy):
        line = jnp.concatenate([ft[x][:, YC * j : YC * (j + 1)] for x in range(CX)], axis=1)
        onehot[:, L * j : L * (j + 1)] = (spots == line).astype(F32).astype(BF16)

    narrow_recv()
    s0, r0, a1, a0 = planes[0], planes[1], planes[2], planes[3]
    s1, r1, a2 = planes[4], planes[5], planes[6]
    lo, hi = yr[0], yr[1]

    def bc(v, n=W):
        return jnp.broadcast_to(v, (CX, n))

    def left(v):
        return pltpu.roll(v, E, 1)

    def right(v):
        return pltpu.roll(v, L - E, 1)

    cor = [[cr[0][CX - 1 :, :], cr[1][CX - 1 :, :]], [cr[2][:1, :], cr[3][:1, :]]]
    edge_u1 = []
    edge_u2 = []
    edge_b1 = []
    for side in range(2):
        hs, hr, h1, h2 = (bc(xr[side, n : n + 1, :]) for n in range(4))
        hu = hs * hr
        at = bc(a0[(CX - 1) * side : (CX - 1) * side + 1, :])
        beside = along_y(hu, left(bc(cor[side][0], L)), right(bc(cor[side][1], L)))
        edge_u1.append(hu)
        edge_b1.append(h1)
        edge_u2.append((hs + h2 + at + h1 + beside) * hr)
    lu2 = lo[0] + left(lo[3]) + right(a0[:, :L]) + lo[2]
    lu2 = (lu2 + along_x(lo[3], bc(cor[0][0], L), bc(cor[1][0], L))) * lo[1]
    hu2 = hi[0] + right(hi[3]) + left(a0[:, W - L :]) + hi[2]
    hu2 = (hu2 + along_x(hi[3], bc(cor[0][1], L), bc(cor[1][1], L))) * hi[1]
    b0 = (s0 + a1 + along_x(a0, edge_u1[0], edge_u1[1]) + along_y(a0, left(lo[3]), right(hi[3]))) * r0
    b1 = (
        s1 + a0 + a2 + along_x(a1, edge_b1[0], edge_b1[1]) + along_y(a1, left(lo[2]), right(hi[2]))
    ) * r1
    face = (s0 + b1 + along_x(b0, edge_u2[0], edge_u2[1]) + along_y(b0, left(lu2), right(hu2))) * r0
    faces[zh, gy] = jnp.concatenate([face[:, : W // 2], face[:, W // 2 :]], axis=0).astype(BF16)

    def ring_d(k):
        half = lax.div(k, 2)
        return n_gy + half * (1 - 2 * lax.rem(k, 2))

    def f_send(k):
        d = ring_d(k)
        bz, by = ring_pos(d)
        return remote(
            faces.at[zh, gy], faces.at[zh, gy], f_ss.at[d], f_rs.at[d], (2 * q + bz, by, gz)
        )

    def f_recv(k):
        d = ring_d(k)
        bz, by = ring_pos(ring - d)
        return remote(
            faces.at[bz, by], faces.at[bz, by], f_ss.at[d], f_rs.at[d], (2 * q + bz, by, gz)
        )

    each(ring, lambda k: f_send(k).start())

    remote(ft, ftr, ft_sem.at[0], ft_sem.at[1], (anti, gy, gz)).wait_recv()
    tables(ftr, 1)
    u_load.wait()
    flat = far * rank
    u_v_all = u_v[...]
    u_p[:flat, :] = dot_nn(u_v_all, onehot[...]).astype(BF16)
    u_p[flat:, :] = jnp.zeros((L - flat, tile), BF16)
    near_load.wait()
    chunk = min(256, tile)
    for n in range(tile // chunk):
        near_p[n * chunk : (n + 1) * chunk, :] = dot_tn(
            near_v[:, n * chunk : (n + 1) * chunk], onehot[...]
        ).astype(BF16)

    rows32 = iota((DZ, W), 0)
    lanes128 = iota((DZ, L), 1)

    def sweep(n, store):
        u = fields[n]

        def step(k, c):
            for j in range(4):
                x = 4 * k + j
                cell = u[x + 1]
                zrow = vzr[n, x]
                up = jnp.where(rows32 == DZ - 1, jnp.where(gz == 0, zrow, 0.0), pltpu.roll(cell, DZ - 1, 0))
                down = jnp.where(rows32 == 0, jnp.where(gz == 0, 0.0, zrow), pltpu.roll(cell, 1, 0))
                low = pltpu.roll(vyr[n, 0, k], (L - E * j) % L, 1)
                high = pltpu.roll(vyr[n, 1, k], (L - E - E * j) % L, 1)
                total = src[x] + u[x] + u[x + 2] + up + down + along_y(cell, low, high)
                store(x, total)
            return c

        lax.fori_loop(0, CX // 4, step, 0)

    def keep(u):
        def store(x, total):
            u[x + 1] = total * rinv[x]

        return store

    each(ring, lambda k: f_recv(k).wait_recv())

    fold = (lax.rem(iota((E, 256), 1), E) == iota((E, 256), 0)).astype(BF16)
    for slot, (half, block) in enumerate(((zh, gx), (1 - zh, anti))):
        flat_faces = faces[half].reshape(16 * n_gy, 256)
        picked = dot_nn(pick[slot], flat_faces).astype(BF16) * mask[slot]
        gath[gz * n_gx + block] = dot_nt(fold, picked).astype(BF16)

    def mine(qq, side):
        return gath.at[pl.ds(side * n_gx + 2 * qq, 2)]

    def g_send(d):
        t = lax.rem(q + d, nq)
        return remote(mine(q, gz), mine(q, gz), g_ss.at[d], g_rs.at[d], (2 * t + zh, gy, gz))

    def g_recv(d):
        s = lax.rem(q + nq - d, nq)
        return remote(mine(s, gz), mine(s, gz), g_ss.at[d], g_rs.at[d], (2 * s + zh, gy, gz))

    def k_send(d):
        s = lax.rem(q + nq - d, nq)
        return remote(mine(s, gz), mine(s, gz), k_ss.at[d], k_rs.at[d], (gx, gy, other))

    def k_recv(d):
        s = lax.rem(q + nq - d, nq)
        return remote(mine(s, other), mine(s, other), k_ss.at[d], k_rs.at[d], (gx, gy, other))

    each(nq, lambda d: g_send(d).start())
    k_send(0).start()

    vol_recv(0)
    sweep(0, keep(u2))
    pack(u2, 1)
    vol_send(1, start)

    v_load.wait()
    each(n_gy, lambda d: vp_recv(d).wait_recv())
    group = lax.div(iota((flat, L), 0), rank)

    def blocks(j, c):
        parts = vparts[j].reshape(flat, L)
        for k in range(far):
            vblk[j, :flat, k * L : (k + 1) * L] = jnp.where(group == k, parts, jnp.zeros_like(parts))
        if flat < L:
            vblk[j, flat:, :] = jnp.zeros((L - flat, far * L), BF16)
        return c

    lax.fori_loop(0, n_gy, blocks, 0)
    each(n_gy, lambda d: col_recv(d).wait_recv())
    to_smem = pltpu.make_async_copy(cols_v, cols_s, smem_sem)
    to_smem.start()
    to_smem.wait()

    def forward(d):
        g_recv(d).wait_recv()
        k_send(d).start()

    each(nq, forward)
    k_recv(0).wait_recv()
    each(nq, lambda d: k_recv(d).wait_recv())

    def w_send(d):
        t = peer(d)
        return remote(ws.at[t], wr.at[gy], w_ss.at[d], w_rs.at[d], (gx, t, gz))

    def w_recv(d):
        s = source_of(d)
        return remote(wr.at[s], wr.at[s], w_ss.at[d], w_rs.at[d], (gx, s, gz))

    def n_send(d):
        t = peer(d)
        return remote(ns.at[t], nr.at[gy], n_ss.at[d], n_rs.at[d], (gx, t, gz))

    def n_recv(d):
        s = source_of(d)
        return remote(nr.at[s], nr.at[s], n_ss.at[d], n_rs.at[d], (gx, s, gz))

    def column(j, k):
        c = cols_s[j, 0, k]
        return gath[lax.rem(c, 2) * n_gx + lax.div(c, 2)]

    def partial_weights(t):
        for k in range(far):
            tsel[:, k * L : (k + 1) * L] = column(t, k + 1)
        return dot_nt(tsel[...], vblk[t])

    def near_out(d):
        t = peer(d)
        ns[t] = column(t, 0)
        n_send(d).start()

    each(n_gy, near_out)
    nr[gy] = column(gy, 0)

    def weights_out(d):
        t = peer(d)
        ws[t] = partial_weights(t)
        w_send(d).start()

    each(n_gy, weights_out)
    wr[gy] = partial_weights(gy)

    vol_recv(1)
    sweep(1, keep(u3))
    pack(u3, 2)
    vol_send(2, start)

    each(n_gy, lambda d: n_recv(d).wait_recv())
    near_t = jnp.concatenate([nr[j] for j in range(n_gy)], axis=1)
    acc = dot_nn(near_t, near_p[...])
    each(n_gy, lambda d: w_recv(d).wait_recv())
    weights = wr[0]
    for j in range(1, n_gy):
        weights = weights + wr[j]
    acc = acc + dot_nn(weights.astype(BF16), u_p[...])
    for j in range(n_gy):
        rs[j] = acc[:, j * L : (j + 1) * L]

    def r_send(d):
        t = peer(d)
        return remote(rs.at[t], rr.at[gy], r_ss.at[d], r_rs.at[d], (gx, t, gz))

    def r_recv(d):
        s = source_of(d)
        return remote(rr.at[s], rr.at[s], r_ss.at[d], r_rs.at[d], (gx, s, gz))

    each(n_gy, lambda d: r_send(d).start())
    rr[gy] = rs[gy]

    def hold(x, total):
        sol[x] = total

    vol_recv(2)
    sweep(2, hold)
    each(n_gy, lambda d: r_recv(d).wait_recv())
    total = rr[0]
    for j in range(1, n_gy):
        total = total + rr[j]
    widen = (iota((E, W), 0) == lax.rem(iota((E, W), 1), E)).astype(F32)
    wide = jnp.dot(total.T, widen, precision=HIGHEST, preferred_element_type=F32)
    keep_cell = lax.rem(iota((L, W), 0), YC) == lax.div(iota((L, W), 1), E)
    value = jnp.sum(jnp.where(keep_cell, wide, 0.0).reshape(CX, YC, W), axis=1)
    face_z = (DZ - 1) * gz
    for x in range(CX):
        line = value[x : x + 1, :]
        flux[x] = line
        sol[x] = (sol[x] + jnp.where(rows32 == face_z, line, 0.0)) * rinv[x]

    x_halo(sent)
    c_halo(sent)
    y_halo(sent)
    ft_copy().wait_send()
    for n in range(3):
        vol_send(n, sent)
    each(n_gy, lambda d: col_send(d).wait_send())
    each(n_gy, lambda d: vp_send(d).wait_send())
    each(ring, lambda k: f_send(k).wait_send())
    each(nq, lambda d: g_send(d).wait_send())
    k_send(0).wait_send()
    each(nq, lambda d: k_send(d).wait_send())
    each(n_gy, lambda d: n_send(d).wait_send())
    each(n_gy, lambda d: w_send(d).wait_send())
    each(n_gy, lambda d: r_send(d).wait_send())


def body(source, coef, face_trace, near_col, far_col, near_tile, far_u, far_v):
    n_gx = lax.axis_size("gx")
    n_gy = lax.axis_size("gy")
    far, rank, tile = far_u.shape[3:]
    total_y = face_trace.shape[2]
    nq, ring, flat = n_gx // 2, 2 * n_gy, far * rank
    cfg = (n_gx, n_gy, far, rank, total_y)
    vmem = pl.BlockSpec(memory_space=pltpu.VMEM)
    smem = pl.BlockSpec(memory_space=pltpu.SMEM)
    anyspace = pl.BlockSpec(memory_space=pl.ANY)
    dma = pltpu.SemaphoreType.DMA
    scratch = [
        pltpu.VMEM((CX + 2, DZ, W), F32),
        pltpu.VMEM((CX + 2, DZ, W), F32),
        pltpu.VMEM((CX + 2, DZ, W), F32),
        pltpu.VMEM((CX, DZ, W), F32),
        pltpu.VMEM((7, CX, W), F32),
        pltpu.VMEM((2, 4, W), F32),
        pltpu.VMEM((2, 4, W), F32),
        pltpu.VMEM((2, 4, CX, L), F32),
        pltpu.VMEM((2, 4, CX, L), F32),
        pltpu.VMEM((4, CX, L), F32),
        pltpu.VMEM((3, 2, CX // 4, DZ, L), F32),
        pltpu.VMEM((3, 2, CX // 4, DZ, L), F32),
        pltpu.VMEM((3, CX, 1, W), F32),
        pltpu.VMEM((3, CX, 1, W), F32),
        pltpu.VMEM((CX, 1, total_y), I32),
        pltpu.VMEM((n_gy, 8, L), I32),
        pltpu.SMEM((n_gy, 8, L), I32),
        pltpu.VMEM((2, L, 16 * n_gy), BF16),
        pltpu.VMEM((2, L, 256), BF16),
        pltpu.VMEM((2, n_gy, 16, 256), BF16),
        pltpu.VMEM((2 * n_gx, E, L), BF16),
        pltpu.VMEM((tile, tile), BF16),
        pltpu.VMEM((tile, tile), BF16),
        pltpu.VMEM((tile, tile), BF16),
        pltpu.VMEM((flat, tile), BF16),
        pltpu.VMEM((L, tile), BF16),
        pltpu.VMEM((n_gy, far, rank, L), BF16),
        pltpu.VMEM((n_gy, L, far * L), BF16),
        pltpu.VMEM((E, far * L), BF16),
        pltpu.VMEM((n_gy, E, L), BF16),
        pltpu.VMEM((n_gy, E, L), BF16),
        pltpu.VMEM((n_gy, E, L), F32),
        pltpu.VMEM((n_gy, E, L), F32),
        pltpu.VMEM((n_gy, E, L), F32),
        pltpu.VMEM((n_gy, E, L), F32),
        dma((3,)),
        dma((4,)), dma((4,)),
        dma((4,)), dma((4,)),
        dma((3, 5)), dma((3, 5)),
        dma((2,)),
        dma((n_gy,)), dma((n_gy,)),
        dma,
        dma((ring,)), dma((ring,)),
        dma((nq,)), dma((nq,)),
        dma((nq,)), dma((nq,)),
        dma((n_gy,)), dma((n_gy,)),
        dma((n_gy,)), dma((n_gy,)),
        dma((n_gy,)), dma((n_gy,)),
        dma((n_gy,)), dma((n_gy,)),
    ]
    return pl.pallas_call(
        functools.partial(kernel, cfg),
        out_shape=(
            jax.ShapeDtypeStruct(source.shape, F32),
            jax.ShapeDtypeStruct((CX, 1, W), F32),
        ),
        in_specs=[smem, smem, vmem, vmem, vmem, anyspace, anyspace, anyspace],
        out_specs=(vmem, vmem),
        scratch_shapes=scratch,
        compiler_params=pltpu.CompilerParams(
            collective_id=0, has_side_effects=True, vmem_limit_bytes=48 * 1024 * 1024
        ),
        name="coupled_step",
    )(
        near_col.reshape(1),
        far_col.reshape(far),
        source,
        coef,
        face_trace,
        near_tile.reshape(tile, tile),
        far_u.reshape(flat, tile),
        far_v.reshape(far, rank, tile),
    )


def solution(mesh):
    return jax.shard_map(
        body,
        mesh=mesh,
        in_specs=(
            P("gx", "gz", "gy"),
            P("gx", "gz", "gy"),
            P("gx", "gz", None),
            P("gx", "gz", "gy"),
            P("gx", "gz", "gy", None),
            P("gx", "gz", "gy", None, None),
            P("gx", "gz", "gy", None, None, None),
            P("gx", "gz", "gy", None, None, None),
        ),
        out_specs=(P("gx", "gz", "gy"), P("gx", "gz", "gy")),
        check_vma=False,
    )
```

```python
import functools

import jax
import jax.numpy as jnp
from jax import lax
from jax.experimental import pallas as pl
from jax.experimental.pallas import tpu as pltpu
from jax.sharding import PartitionSpec as P

E = 32
CX = 8
YC = 16
DZ = 32
W = YC * E
L = 128
F32 = jnp.float32
BF16 = jnp.bfloat16
I32 = jnp.int32
TEAM = 4
MESH = pl.DeviceIdType.MESH
HIGHEST = lax.Precision.HIGHEST


def dot_nt(a, b):
    return lax.dot_general(a, b, (((1,), (1,)), ((), ())), preferred_element_type=F32)


def dot_tn(a, b):
    return lax.dot_general(a, b, (((0,), (0,)), ((), ())), preferred_element_type=F32)


def dot_nn(a, b):
    return lax.dot_general(a, b, (((1,), (0,)), ((), ())), preferred_element_type=F32)


def iota(shape, dim):
    return lax.broadcasted_iota(I32, shape, dim)


def along_x(field, low, high):
    rows = iota(field.shape, 0)
    before = jnp.where(rows == 0, low, pltpu.roll(field, 1, 0))
    after = jnp.where(rows == field.shape[0] - 1, high, pltpu.roll(field, field.shape[0] - 1, 0))
    return before + after


def along_y(field, low, high):
    n = field.shape[0]
    lanes = iota((n, L), 1)
    before = pltpu.roll(field, E, 1)
    after = pltpu.roll(field, W - E, 1)
    first = jnp.where(lanes < E, low, before[:, :L])
    last = jnp.where(lanes >= L - E, high, after[:, W - L :])
    before = jnp.concatenate([first, before[:, L:]], axis=1)
    after = jnp.concatenate([after[:, : W - L], last], axis=1)
    return before + after


def kernel(
    cfg,
    ncol_h, fcol_h, src_h, coef_h, ft_h, near_h, u_h, v_h,
    sol, flux,
    ncol, fcol, src, coef, ft,
    u1, u2, u3, rinv, planes,
    xs, xr, ys, yr, cs, cr,
    vxs, vxr, vys, vyr, vzs, vzr,
    ftr, cols_v, cols_s,
    pick, mask, faces, gath,
    near_v, near_p, onehot, u_v, u_p,
    vparts, vblk, tsel, ns, nr, ws, wr, rs, rr,
    load_sem, in_sem, x_ss, x_rs, c_ss, c_rs, v_ss, v_rs, ft_sem, col_ss, col_rs, smem_sem,
    f_ss, f_rs, g_ss, g_rs, k_ss, k_rs, vp_ss, vp_rs, n_ss, n_rs, w_ss, w_rs, r_ss, r_rs,
):
    n_gx, n_gy, far, rank, total_y = cfg
    tile = CX * total_y
    team = min(TEAM, n_gy)
    part = tile // team
    nq = n_gx // 2
    ring = 2 * n_gy
    gx = lax.axis_index("gx")
    gy = lax.axis_index("gy")
    gz = lax.axis_index("gz")
    zh = lax.rem(gx, 2)
    q = lax.div(gx, 2)
    anti = gx + 1 - 2 * zh
    other = 1 - gz
    me = zh * n_gy + gy
    seat = lax.rem(gy, team)
    bench = gy - seat
    low_x, high_x = gx > 0, gx < n_gx - 1
    low_y, high_y = gy > 0, gy < n_gy - 1

    def remote(a, b, ssem, rsem, dev):
        return pltpu.make_async_remote_copy(
            src_ref=a, dst_ref=b, send_sem=ssem, recv_sem=rsem, device_id=dev, device_id_type=MESH
        )

    bar = pltpu.get_barrier_semaphore()

    def signal(x, y, z):
        pl.semaphore_signal(bar, inc=1, device_id=(x, y, z), device_id_type=MESH)

    count = ring - 1 + nq - 1 + 1
    for dx, hx in ((-1, low_x), (1, high_x)):
        for dy, hy in ((-1, low_y), (0, None), (1, high_y)):
            cond = hx if hy is None else jnp.logical_and(hx, hy)
            count = count + cond.astype(I32)

            @pl.when(cond)
            def _(dx=dx, dy=dy):
                signal(gx + dx, gy + dy, gz)

    def ring_pos(d):
        pos = lax.rem(me + d, ring)
        return lax.div(pos, n_gy), lax.rem(pos, n_gy)

    def ring_signal(d, c):
        bz, by = ring_pos(d)
        signal(2 * q + bz, by, gz)
        return c

    lax.fori_loop(1, ring, ring_signal, 0)

    def xy_signal(d, c):
        signal(2 * lax.rem(q + d, nq) + zh, gy, gz)
        return c

    lax.fori_loop(1, nq, xy_signal, 0)
    signal(gx, gy, other)

    loads = [
        pltpu.make_async_copy(a, b, in_sem.at[n])
        for n, (a, b) in enumerate(
            ((coef_h, coef), (src_h, src), (ft_h, ft), (ncol_h, ncol), (fcol_h, fcol))
        )
    ]
    for load in loads:
        load.start()
    near_load = pltpu.make_async_copy(near_h, near_v, load_sem.at[0])
    u_load = pltpu.make_async_copy(u_h, u_v, load_sem.at[1])
    v_load = pltpu.make_async_copy(
        v_h.at[:, :, pl.ds(pl.multiple_of(seat * part, L), part)], vparts.at[seat], load_sem.at[2]
    )
    near_load.start()
    u_load.start()
    v_load.start()

    spread = (iota((YC, W), 0) == lax.div(iota((YC, W), 1), E)).astype(F32)

    def first(x, c):
        wide = lax.dot_general(
            coef[x], spread, (((0,), (0,)), ((), ())),
            precision=HIGHEST, preferred_element_type=F32,
        )
        r = 1.0 / (6.0 + wide)
        rinv[x] = r
        u1[x + 1] = src[x] * r
        return c

    for load in loads:
        load.wait()
    lax.fori_loop(0, CX, first, 0)

    rows8 = iota((CX, W), 0)

    def plane(ref, off, depth):
        out = jnp.zeros((CX, W), F32)
        for x in range(CX):
            row = jnp.where(
                gz == 0,
                ref[x + off, depth : depth + 1, :],
                ref[x + off, DZ - 1 - depth : DZ - depth, :],
            )
            out = jnp.where(rows8 == x, row, out)
        return out

    for n, (ref, off, depth) in enumerate(
        ((src, 0, 0), (rinv, 0, 0), (u1, 1, 1), (u1, 1, 0), (src, 0, 1), (rinv, 0, 1), (u1, 1, 2))
    ):
        planes[n] = plane(ref, off, depth)
    for side, (edge, inner, lane) in enumerate(((0, 1, 0), (CX - 1, CX - 2, W - L))):
        for n in range(3):
            xs[side, n : n + 1, :] = planes[n, edge : edge + 1, :]
        xs[side, 3:4, :] = planes[3, inner : inner + 1, :]
        for n in range(4):
            ys[side, n] = planes[n, :, lane : lane + L]
        for b, lane_b in enumerate((0, W - L)):
            cs[2 * side + b] = planes[3, edge : edge + 1, lane_b : lane_b + L]

    lanes_col = iota((8, L), 1)
    row = jnp.where(lanes_col == 0, ncol[0, 0, 0], 0)
    for k in range(far):
        row = jnp.where(lanes_col == k + 1, fcol[0, 0, 0, k], row)
    cols_v[seat] = row

    lanes32 = lax.div(iota((DZ, L), 1), E)

    def pack(u, n):
        if n == 1:
            vxs[0] = u[1].astype(BF16)
            vxs[1] = u[CX].astype(BF16)

        def step(k, c):
            low = jnp.zeros((DZ, L), F32)
            high = jnp.zeros((DZ, L), F32)
            for j in range(4):
                cell = u[4 * k + j + 1]
                low = jnp.where(lanes32 == j, pltpu.roll(cell[:, :L], E * j, 1), low)
                high = jnp.where(
                    lanes32 == j, pltpu.roll(cell[:, W - L :], (E * j - (L - E)) % L, 1), high
                )
            vys[n, 0, k] = low
            vys[n, 1, k] = high
            return c

        lax.fori_loop(0, CX // 4, step, 0)

        def zstep(x, c):
            vzs[n, x] = jnp.where(gz == 0, u[x + 1, DZ - 1 : DZ, :], u[x + 1, 0:1, :])
            return c

        lax.fori_loop(0, CX, zstep, 0)

    pack(u1, 0)

    for side, have in ((0, low_x), (1, high_x)):

        @pl.when(jnp.logical_not(have))
        def _(side=side):
            xr[side] = jnp.zeros((4, W), F32)
            for u in (u1, u2, u3):
                u[side * (CX + 1)] = jnp.zeros((DZ, W), F32)

    for side, have in ((0, low_y), (1, high_y)):

        @pl.when(jnp.logical_not(have))
        def _(side=side):
            yr[side] = jnp.zeros((4, CX, L), F32)
            for n in range(3):
                vyr[n, side] = jnp.zeros((CX // 4, DZ, L), F32)

    for a, hx in ((0, low_x), (1, high_x)):
        for b, hy in ((0, low_y), (1, high_y)):

            @pl.when(jnp.logical_not(jnp.logical_and(hx, hy)))
            def _(a=a, b=b):
                cr[2 * a + b] = jnp.zeros((1, L), F32)

    pl.semaphore_wait(bar, count)

    sides = ((0, low_x, -1), (1, high_x, 1))
    sides_y = ((0, low_y, -1), (1, high_y, 1))

    def x_copy(side, dx):
        return remote(xs.at[side], xr.at[1 - side], x_ss.at[side], x_rs.at[1 - side], (gx + dx, gy, gz))

    def y_copy(side, dy):
        return remote(
            ys.at[side], yr.at[1 - side], x_ss.at[2 + side], x_rs.at[3 - side], (gx, gy + dy, gz)
        )

    def c_copy(a, dx, b, dy):
        there = 2 * (1 - a) + 1 - b
        return remote(
            cs.at[2 * a + b], cr.at[there], c_ss.at[2 * a + b], c_rs.at[there], (gx + dx, gy + dy, gz)
        )

    def x_halo(act):
        for side, have, dx in sides:

            @pl.when(have)
            def _(side=side, dx=dx):
                act(x_copy(side, dx), 0)

    def c_halo(act):
        for a, hx, dx in sides:
            for b, hy, dy in sides_y:

                @pl.when(jnp.logical_and(hx, hy))
                def _(a=a, dx=dx, b=b, dy=dy):
                    act(c_copy(a, dx, b, dy), 0)

    def y_halo(act):
        for side, have, dy in sides_y:

            @pl.when(have)
            def _(side=side, dy=dy):
                act(y_copy(side, dy), 0)

    def narrow_recv():
        for side, have, dx in sides:

            @pl.when(have)
            def _(side=side, dx=dx):
                remote(
                    xs.at[side], xr.at[side], x_ss.at[side], x_rs.at[side], (gx + dx, gy, gz)
                ).wait_recv()

        for side, have, dy in sides_y:

            @pl.when(have)
            def _(side=side, dy=dy):
                remote(
                    ys.at[side], yr.at[side], x_ss.at[2 + side], x_rs.at[2 + side], (gx, gy + dy, gz)
                ).wait_recv()

        for a, hx, dx in sides:
            for b, hy, dy in sides_y:

                @pl.when(jnp.logical_and(hx, hy))
                def _(a=a, dx=dx, b=b, dy=dy):
                    remote(
                        cs.at[2 * a + b], cr.at[2 * a + b], c_ss.at[2 * a + b], c_rs.at[2 * a + b],
                        (gx + dx, gy + dy, gz),
                    ).wait_recv()

    def start(copy, _):
        copy.start()

    def sent(copy, _):
        copy.wait_send()

    x_halo(start)
    c_halo(start)
    y_halo(start)

    def ft_copy():
        return remote(ft, ftr, ft_sem.at[0], ft_sem.at[1], (anti, gy, gz))

    ft_copy().start()

    def peer(d):
        return lax.rem(gy + d, n_gy)

    def source_of(d):
        return lax.rem(gy + n_gy - d, n_gy)

    def mate(d):
        return lax.rem(seat + d, team)

    def mate_from(d):
        return lax.rem(seat + team - d, team)

    def col_send(d):
        return remote(
            cols_v.at[seat], cols_v.at[seat], col_ss.at[d], col_rs.at[d], (gx, bench + mate(d), gz)
        )

    def col_recv(d):
        s = mate_from(d)
        return remote(cols_v.at[s], cols_v.at[s], col_ss.at[d], col_rs.at[d], (gx, bench + s, gz))

    def vp_send(d):
        t = mate(d)
        return remote(
            v_h.at[:, :, pl.ds(pl.multiple_of(t * part, L), part)], vparts.at[seat],
            vp_ss.at[d], vp_rs.at[d], (gx, bench + t, gz),
        )

    def vp_recv(d):
        s = mate_from(d)
        return remote(vparts.at[s], vparts.at[s], vp_ss.at[d], vp_rs.at[d], (gx, bench + s, gz))

    def each(n, f):
        def step(d, c):
            f(d)
            return c

        lax.fori_loop(1, n, step, 0)

    each(team, lambda d: col_send(d).start())

    fields = (u1, u2, u3)

    def vol_send(n, act):
        u = fields[n]
        for side, have, dx in sides:

            @pl.when(have)
            def _(side=side, dx=dx):
                out = vxs.at[side] if n == 1 else u.at[1 + side * (CX - 1)]
                there = vxr.at[1 - side] if n == 1 else u.at[(1 - side) * (CX + 1)]
                act(
                    remote(
                        out, there,
                        v_ss.at[n, side], v_rs.at[n, 1 - side], (gx + dx, gy, gz),
                    ),
                    0,
                )

        for side, have, dy in sides_y:

            @pl.when(have)
            def _(side=side, dy=dy):
                act(
                    remote(
                        vys.at[n, side], vyr.at[n, 1 - side],
                        v_ss.at[n, 2 + side], v_rs.at[n, 3 - side], (gx, gy + dy, gz),
                    ),
                    0,
                )

        act(remote(vzs.at[n], vzr.at[n], v_ss.at[n, 4], v_rs.at[n, 4], (gx, gy, other)), 0)

    def vol_recv(n):
        u = fields[n]
        for side, have, dx in sides:

            @pl.when(have)
            def _(side=side, dx=dx):
                halo = vxr.at[side] if n == 1 else u.at[side * (CX + 1)]
                remote(halo, halo, v_ss.at[n, side], v_rs.at[n, side], (gx + dx, gy, gz)).wait_recv()
                if n == 1:
                    u[side * (CX + 1)] = vxr[side].astype(F32)

        for side, have, dy in sides_y:

            @pl.when(have)
            def _(side=side, dy=dy):
                halo = vyr.at[n, side]
                remote(
                    halo, halo, v_ss.at[n, 2 + side], v_rs.at[n, 2 + side], (gx, gy + dy, gz)
                ).wait_recv()

        remote(vzr.at[n], vzr.at[n], v_ss.at[n, 4], v_rs.at[n, 4], (gx, gy, other)).wait_recv()

    vol_send(0, start)

    def tables(table, slot):
        spot = iota((part, total_y), 0) + seat * part
        col = iota((part, total_y), 1)
        cell = jnp.zeros((part, total_y), I32)
        for x in range(CX):
            cell = jnp.where(table[x] == spot, col + x * total_y, cell)
        cell = jnp.sum(cell.astype(F32), axis=1, keepdims=True).astype(I32)
        x = lax.div(cell, total_y)
        y = cell - x * total_y
        y8 = lax.div(y, 8)
        pick[slot] = (iota((part, 16 * n_gy), 1) == y8 * 8 + x).astype(BF16)
        mask[slot] = (lax.div(iota((part, 256), 1), E) == y - y8 * 8).astype(BF16)

    tables(ft, 0)
    spots = iota((tile, L), 0)
    for j in range(n_gy):
        line = jnp.concatenate([ft[x][:, YC * j : YC * (j + 1)] for x in range(CX)], axis=1)
        onehot[:, L * j : L * (j + 1)] = (spots == line).astype(F32).astype(BF16)

    narrow_recv()
    s0, r0, a1, a0 = planes[0], planes[1], planes[2], planes[3]
    s1, r1, a2 = planes[4], planes[5], planes[6]
    lo, hi = yr[0], yr[1]

    def bc(v, n=W):
        return jnp.broadcast_to(v, (CX, n))

    def left(v):
        return pltpu.roll(v, E, 1)

    def right(v):
        return pltpu.roll(v, L - E, 1)

    cor = [[cr[0], cr[1]], [cr[2], cr[3]]]
    edge_u1 = []
    edge_u2 = []
    edge_b1 = []
    for side in range(2):
        hs, hr, h1, h2 = (bc(xr[side, n : n + 1, :]) for n in range(4))
        hu = hs * hr
        at = bc(a0[(CX - 1) * side : (CX - 1) * side + 1, :])
        beside = along_y(hu, left(bc(cor[side][0], L)), right(bc(cor[side][1], L)))
        edge_u1.append(hu)
        edge_b1.append(h1)
        edge_u2.append((hs + h2 + at + h1 + beside) * hr)
    lu2 = lo[0] + left(lo[3]) + right(a0[:, :L]) + lo[2]
    lu2 = (lu2 + along_x(lo[3], bc(cor[0][0], L), bc(cor[1][0], L))) * lo[1]
    hu2 = hi[0] + right(hi[3]) + left(a0[:, W - L :]) + hi[2]
    hu2 = (hu2 + along_x(hi[3], bc(cor[0][1], L), bc(cor[1][1], L))) * hi[1]
    b0 = (s0 + a1 + along_x(a0, edge_u1[0], edge_u1[1]) + along_y(a0, left(lo[3]), right(hi[3]))) * r0
    b1 = (
        s1 + a0 + a2 + along_x(a1, edge_b1[0], edge_b1[1]) + along_y(a1, left(lo[2]), right(hi[2]))
    ) * r1
    face = (s0 + b1 + along_x(b0, edge_u2[0], edge_u2[1]) + along_y(b0, left(lu2), right(hu2))) * r0
    faces[zh, gy] = jnp.concatenate([face[:, : W // 2], face[:, W // 2 :]], axis=0).astype(BF16)

    def ring_d(k):
        half = lax.div(k, 2)
        return n_gy + half * (1 - 2 * lax.rem(k, 2))

    def f_send(k):
        d = ring_d(k)
        bz, by = ring_pos(d)
        return remote(
            faces.at[zh, gy], faces.at[zh, gy], f_ss.at[d], f_rs.at[d], (2 * q + bz, by, gz)
        )

    def f_recv(k):
        d = ring_d(k)
        bz, by = ring_pos(ring - d)
        return remote(
            faces.at[bz, by], faces.at[bz, by], f_ss.at[d], f_rs.at[d], (2 * q + bz, by, gz)
        )

    each(ring, lambda k: f_send(k).start())

    each(team, lambda d: vp_send(d).start())

    remote(ft, ftr, ft_sem.at[0], ft_sem.at[1], (anti, gy, gz)).wait_recv()
    tables(ftr, 1)
    u_load.wait()
    flat = far * rank
    u_v_all = u_v[...]
    u_p[:flat, :] = dot_nn(u_v_all, onehot[...]).astype(BF16)
    u_p[flat:, :] = jnp.zeros((L - flat, tile), BF16)
    near_load.wait()
    chunk = min(256, tile)
    for n in range(tile // chunk):
        near_p[n * chunk : (n + 1) * chunk, :] = dot_tn(
            near_v[:, n * chunk : (n + 1) * chunk], onehot[...]
        ).astype(BF16)

    rows32 = iota((DZ, W), 0)
    lanes128 = iota((DZ, L), 1)

    def sweep(n, store):
        u = fields[n]

        def step(k, c):
            for j in range(4):
                x = 4 * k + j
                cell = u[x + 1]
                zrow = vzr[n, x]
                up = jnp.where(rows32 == DZ - 1, jnp.where(gz == 0, zrow, 0.0), pltpu.roll(cell, DZ - 1, 0))
                down = jnp.where(rows32 == 0, jnp.where(gz == 0, 0.0, zrow), pltpu.roll(cell, 1, 0))
                low = pltpu.roll(vyr[n, 0, k], (L - E * j) % L, 1)
                high = pltpu.roll(vyr[n, 1, k], (L - E - E * j) % L, 1)
                total = src[x] + u[x] + u[x + 2] + up + down + along_y(cell, low, high)
                store(x, total)
            return c

        lax.fori_loop(0, CX // 4, step, 0)

    def keep(u):
        def store(x, total):
            u[x + 1] = total * rinv[x]

        return store

    each(team, lambda d: col_recv(d).wait_recv())
    to_smem = pltpu.make_async_copy(cols_v, cols_s, smem_sem)
    to_smem.start()
    to_smem.wait()

    each(ring, lambda k: f_recv(k).wait_recv())

    fold = (lax.rem(iota((E, 256), 1), E) == iota((E, 256), 0)).astype(BF16)
    for slot, (half, block) in enumerate(((zh, gx), (1 - zh, anti))):
        flat_faces = faces[half].reshape(16 * n_gy, 256)
        picked = dot_nn(pick[slot], flat_faces).astype(BF16) * mask[slot]
        gath[gz * n_gx + block] = dot_nt(fold, picked).astype(BF16)

    def mine(qq, side):
        return gath.at[pl.ds(side * n_gx + 2 * qq, 2)]

    def g_send(d):
        t = lax.rem(q + d, nq)
        return remote(mine(q, gz), mine(q, gz), g_ss.at[d], g_rs.at[d], (2 * t + zh, gy, gz))

    def g_recv(d):
        s = lax.rem(q + nq - d, nq)
        return remote(mine(s, gz), mine(s, gz), g_ss.at[d], g_rs.at[d], (2 * s + zh, gy, gz))

    def k_send(d):
        s = lax.rem(q + nq - d, nq)
        return remote(mine(s, gz), mine(s, gz), k_ss.at[d], k_rs.at[d], (gx, gy, other))

    def k_recv(d):
        s = lax.rem(q + nq - d, nq)
        return remote(mine(s, other), mine(s, other), k_ss.at[d], k_rs.at[d], (gx, gy, other))

    each(nq, lambda d: g_send(d).start())
    k_send(0).start()

    vol_recv(0)
    sweep(0, keep(u2))
    pack(u2, 1)
    vol_send(1, start)

    v_load.wait()
    each(team, lambda d: vp_recv(d).wait_recv())
    group = lax.div(iota((flat, part), 0), rank)

    def blocks(j, c):
        parts = vparts[j].reshape(flat, part)
        for k in range(far):
            vblk[j, :flat, k * part : (k + 1) * part] = jnp.where(group == k, parts, jnp.zeros_like(parts))
        if flat < L:
            vblk[j, flat:, :] = jnp.zeros((L - flat, far * part), BF16)
        return c

    lax.fori_loop(0, team, blocks, 0)

    def forward(d):
        g_recv(d).wait_recv()
        k_send(d).start()

    each(nq, forward)
    k_recv(0).wait_recv()
    each(nq, lambda d: k_recv(d).wait_recv())

    def w_send(d):
        t = mate(d)
        return remote(ws.at[t], wr.at[seat], w_ss.at[d], w_rs.at[d], (gx, bench + t, gz))

    def w_recv(d):
        s = mate_from(d)
        return remote(wr.at[s], wr.at[s], w_ss.at[d], w_rs.at[d], (gx, bench + s, gz))

    def n_send(d):
        t = mate(d)
        return remote(ns.at[t], nr.at[seat], n_ss.at[d], n_rs.at[d], (gx, bench + t, gz))

    def n_recv(d):
        s = mate_from(d)
        return remote(nr.at[s], nr.at[s], n_ss.at[d], n_rs.at[d], (gx, bench + s, gz))

    def column(j, k):
        c = cols_s[j, 0, k]
        return gath[lax.rem(c, 2) * n_gx + lax.div(c, 2)]

    def partial_weights(t):
        for k in range(far):
            tsel[:, k * part : (k + 1) * part] = column(t, k + 1)
        return dot_nt(tsel[...], vblk[t])

    def near_out(d):
        t = mate(d)
        ns[t] = column(t, 0)
        n_send(d).start()

    each(team, near_out)
    nr[seat] = column(seat, 0)

    def weights_out(d):
        t = mate(d)
        ws[t] = partial_weights(t)
        w_send(d).start()

    each(team, weights_out)
    wr[seat] = partial_weights(seat)

    vol_recv(1)
    sweep(1, keep(u3))
    pack(u3, 2)
    vol_send(2, start)

    each(team, lambda d: n_recv(d).wait_recv())
    near_t = jnp.concatenate([nr[j] for j in range(team)], axis=1)
    acc = dot_nn(near_t, near_p[...])
    each(team, lambda d: w_recv(d).wait_recv())
    weights = wr[0]
    for j in range(1, team):
        weights = weights + wr[j]
    acc = acc + dot_nn(weights.astype(BF16), u_p[...])
    for j in range(n_gy):
        rs[j] = acc[:, j * L : (j + 1) * L]

    def r_send(d):
        t = peer(d)
        return remote(rs.at[t], rr.at[gy], r_ss.at[d], r_rs.at[d], (gx, t, gz))

    def r_recv(d):
        s = source_of(d)
        return remote(rr.at[s], rr.at[s], r_ss.at[d], r_rs.at[d], (gx, s, gz))

    each(n_gy, lambda d: r_send(d).start())
    rr[gy] = rs[gy]

    def hold(x, total):
        sol[x] = total

    x_halo(sent)
    c_halo(sent)
    y_halo(sent)
    ft_copy().wait_send()
    each(team, lambda d: col_send(d).wait_send())
    each(team, lambda d: vp_send(d).wait_send())
    each(ring, lambda k: f_send(k).wait_send())
    each(nq, lambda d: g_send(d).wait_send())
    k_send(0).wait_send()
    each(nq, lambda d: k_send(d).wait_send())
    each(team, lambda d: n_send(d).wait_send())
    each(team, lambda d: w_send(d).wait_send())
    for n in range(3):
        vol_send(n, sent)
    vol_recv(2)
    sweep(2, hold)
    each(n_gy, lambda d: r_recv(d).wait_recv())
    total = rr[0]
    for j in range(1, n_gy):
        total = total + rr[j]
    widen = (iota((E, W), 0) == lax.rem(iota((E, W), 1), E)).astype(F32)
    wide = jnp.dot(total.T, widen, precision=HIGHEST, preferred_element_type=F32)
    keep_cell = lax.rem(iota((L, W), 0), YC) == lax.div(iota((L, W), 1), E)
    value = jnp.sum(jnp.where(keep_cell, wide, 0.0).reshape(CX, YC, W), axis=1)
    face_z = (DZ - 1) * gz
    for x in range(CX):
        line = value[x : x + 1, :]
        flux[x] = line
        sol[x] = (sol[x] + jnp.where(rows32 == face_z, line, 0.0)) * rinv[x]

    each(n_gy, lambda d: r_send(d).wait_send())


def body(source, coef, face_trace, near_col, far_col, near_tile, far_u, far_v):
    n_gx = lax.axis_size("gx")
    n_gy = lax.axis_size("gy")
    far, rank, tile = far_u.shape[3:]
    total_y = face_trace.shape[2]
    nq, ring, flat = n_gx // 2, 2 * n_gy, far * rank
    team = min(TEAM, n_gy)
    part = tile // team
    cfg = (n_gx, n_gy, far, rank, total_y)
    vmem = pl.BlockSpec(memory_space=pltpu.VMEM)
    anyspace = pl.BlockSpec(memory_space=pl.ANY)
    dma = pltpu.SemaphoreType.DMA
    scratch = [
        pltpu.SMEM((1, 1, 1), I32),
        pltpu.SMEM((1, 1, 1, far), I32),
        pltpu.VMEM((CX, DZ, W), F32),
        pltpu.VMEM((CX, YC, DZ), F32),
        pltpu.VMEM((CX, 1, total_y), I32),
        pltpu.VMEM((CX + 2, DZ, W), F32),
        pltpu.VMEM((CX + 2, DZ, W), F32),
        pltpu.VMEM((CX + 2, DZ, W), F32),
        pltpu.VMEM((CX, DZ, W), F32),
        pltpu.VMEM((7, CX, W), F32),
        pltpu.VMEM((2, 4, W), F32),
        pltpu.VMEM((2, 4, W), F32),
        pltpu.VMEM((2, 4, CX, L), F32),
        pltpu.VMEM((2, 4, CX, L), F32),
        pltpu.VMEM((4, 1, L), F32),
        pltpu.VMEM((4, 1, L), F32),
        pltpu.VMEM((2, DZ, W), BF16),
        pltpu.VMEM((2, DZ, W), BF16),
        pltpu.VMEM((3, 2, CX // 4, DZ, L), F32),
        pltpu.VMEM((3, 2, CX // 4, DZ, L), F32),
        pltpu.VMEM((3, CX, 1, W), F32),
        pltpu.VMEM((3, CX, 1, W), F32),
        pltpu.VMEM((CX, 1, total_y), I32),
        pltpu.VMEM((team, 8, L), I32),
        pltpu.SMEM((team, 8, L), I32),
        pltpu.VMEM((2, part, 16 * n_gy), BF16),
        pltpu.VMEM((2, part, 256), BF16),
        pltpu.VMEM((2, n_gy, 16, 256), BF16),
        pltpu.VMEM((2 * n_gx, E, part), BF16),
        pltpu.VMEM((tile, tile), BF16),
        pltpu.VMEM((tile, tile), BF16),
        pltpu.VMEM((tile, tile), BF16),
        pltpu.VMEM((flat, tile), BF16),
        pltpu.VMEM((L, tile), BF16),
        pltpu.VMEM((team, far, rank, part), BF16),
        pltpu.VMEM((team, L, far * part), BF16),
        pltpu.VMEM((E, far * part), BF16),
        pltpu.VMEM((team, E, part), BF16),
        pltpu.VMEM((team, E, part), BF16),
        pltpu.VMEM((team, E, L), F32),
        pltpu.VMEM((team, E, L), F32),
        pltpu.VMEM((n_gy, E, L), F32),
        pltpu.VMEM((n_gy, E, L), F32),
        dma((3,)),
        dma((5,)),
        dma((4,)), dma((4,)),
        dma((4,)), dma((4,)),
        dma((3, 5)), dma((3, 5)),
        dma((2,)),
        dma((n_gy,)), dma((n_gy,)),
        dma,
        dma((ring,)), dma((ring,)),
        dma((nq,)), dma((nq,)),
        dma((nq,)), dma((nq,)),
        dma((n_gy,)), dma((n_gy,)),
        dma((n_gy,)), dma((n_gy,)),
        dma((n_gy,)), dma((n_gy,)),
        dma((n_gy,)), dma((n_gy,)),
    ]
    return pl.pallas_call(
        functools.partial(kernel, cfg),
        out_shape=(
            jax.ShapeDtypeStruct(source.shape, F32),
            jax.ShapeDtypeStruct((CX, 1, W), F32),
        ),
        in_specs=[anyspace] * 8,
        out_specs=(vmem, vmem),
        scratch_shapes=scratch,
        compiler_params=pltpu.CompilerParams(
            collective_id=0, has_side_effects=True, vmem_limit_bytes=60 * 1024 * 1024
        ),
        name="coupled_step",
    )(
        near_col,
        far_col,
        source,
        coef.swapaxes(1, 2),
        face_trace,
        near_tile.reshape(tile, tile),
        far_u.reshape(flat, tile),
        far_v.reshape(far, rank, tile),
    )


def solution(mesh):
    return jax.shard_map(
        body,
        mesh=mesh,
        in_specs=(
            P("gx", "gz", "gy"),
            P("gx", "gz", "gy"),
            P("gx", "gz", None),
            P("gx", "gz", "gy"),
            P("gx", "gz", "gy", None),
            P("gx", "gz", "gy", None, None),
            P("gx", "gz", "gy", None, None, None),
            P("gx", "gz", "gy", None, None, None),
        ),
        out_specs=(P("gx", "gz", "gy"), P("gx", "gz", "gy")),
        check_vma=False,
    )
```

```python
import functools

import jax
import jax.numpy as jnp
from jax import lax
from jax.experimental import pallas as pl
from jax.experimental.pallas import tpu as pltpu
from jax.sharding import PartitionSpec as P

E = 32
CX = 8
YC = 16
DZ = 32
W = YC * E
L = 128
F32 = jnp.float32
BF16 = jnp.bfloat16
I32 = jnp.int32
TEAM = 4
MESH = pl.DeviceIdType.MESH
HIGHEST = lax.Precision.HIGHEST


def dot_nt(a, b):
    return lax.dot_general(a, b, (((1,), (1,)), ((), ())), preferred_element_type=F32)


def dot_tn(a, b):
    return lax.dot_general(a, b, (((0,), (0,)), ((), ())), preferred_element_type=F32)


def dot_nn(a, b):
    return lax.dot_general(a, b, (((1,), (0,)), ((), ())), preferred_element_type=F32)


def iota(shape, dim):
    return lax.broadcasted_iota(I32, shape, dim)


def along_x(field, low, high):
    rows = iota(field.shape, 0)
    before = jnp.where(rows == 0, low, pltpu.roll(field, 1, 0))
    after = jnp.where(rows == field.shape[0] - 1, high, pltpu.roll(field, field.shape[0] - 1, 0))
    return before + after


def along_y(field, low, high):
    n = field.shape[0]
    lanes = iota((n, L), 1)
    before = pltpu.roll(field, E, 1)
    after = pltpu.roll(field, W - E, 1)
    first = jnp.where(lanes < E, low, before[:, :L])
    last = jnp.where(lanes >= L - E, high, after[:, W - L :])
    before = jnp.concatenate([first, before[:, L:]], axis=1)
    after = jnp.concatenate([after[:, : W - L], last], axis=1)
    return before + after


def kernel(
    cfg,
    ncol_h, fcol_h, src_h, coef_h, ft_h, near_h, u_h, v_h,
    sol, flux,
    ncol, fcol, src, coef, ft,
    u1, u2, u3, rinv, planes,
    xs, xr, ys, yr, cs, cr,
    vxs, vxr, vys, vyr, vzs, vzr,
    ftr, cols_v, cols_s,
    pick, mask, faces, gath,
    near_v, near_p, onehot, u_v, u_p,
    vparts, vblk, tsel, ns, nr, ws, wr, rs, rr,
    load_sem, in_sem, x_ss, x_rs, c_ss, c_rs, v_ss, v_rs, ft_sem, col_ss, col_rs, smem_sem,
    f_ss, f_rs, g_ss, g_rs, k_ss, k_rs, vp_ss, vp_rs, n_ss, n_rs, w_ss, w_rs, r_ss, r_rs,
):
    n_gx, n_gy, far, rank, total_y = cfg
    tile = CX * total_y
    team = min(TEAM, n_gy)
    part = tile // team
    nq = n_gx // 2
    ring = 2 * n_gy
    gx = lax.axis_index("gx")
    gy = lax.axis_index("gy")
    gz = lax.axis_index("gz")
    zh = lax.rem(gx, 2)
    q = lax.div(gx, 2)
    anti = gx + 1 - 2 * zh
    other = 1 - gz
    me = zh * n_gy + gy
    seat = lax.rem(gy, team)
    bench = gy - seat
    low_x, high_x = gx > 0, gx < n_gx - 1
    low_y, high_y = gy > 0, gy < n_gy - 1

    def remote(a, b, ssem, rsem, dev):
        return pltpu.make_async_remote_copy(
            src_ref=a, dst_ref=b, send_sem=ssem, recv_sem=rsem, device_id=dev, device_id_type=MESH
        )

    bar = pltpu.get_barrier_semaphore()

    def signal(x, y, z):
        pl.semaphore_signal(bar, inc=1, device_id=(x, y, z), device_id_type=MESH)

    count = ring - 1 + nq - 1 + 1
    for dx, hx in ((-1, low_x), (1, high_x)):
        for dy, hy in ((-1, low_y), (0, None), (1, high_y)):
            cond = hx if hy is None else jnp.logical_and(hx, hy)
            count = count + cond.astype(I32)

            @pl.when(cond)
            def _(dx=dx, dy=dy):
                signal(gx + dx, gy + dy, gz)

    def ring_pos(d):
        pos = lax.rem(me + d, ring)
        return lax.div(pos, n_gy), lax.rem(pos, n_gy)

    def ring_signal(d, c):
        bz, by = ring_pos(d)
        signal(2 * q + bz, by, gz)
        return c

    lax.fori_loop(1, ring, ring_signal, 0)

    def xy_signal(d, c):
        signal(2 * lax.rem(q + d, nq) + zh, gy, gz)
        return c

    lax.fori_loop(1, nq, xy_signal, 0)
    signal(gx, gy, other)

    loads = [
        pltpu.make_async_copy(a, b, in_sem.at[n])
        for n, (a, b) in enumerate(
            ((coef_h, coef), (src_h, src), (ft_h, ft), (ncol_h, ncol), (fcol_h, fcol))
        )
    ]
    for load in loads:
        load.start()
    near_load = pltpu.make_async_copy(near_h, near_v, load_sem.at[0])
    u_load = pltpu.make_async_copy(u_h, u_v, load_sem.at[1])
    v_load = pltpu.make_async_copy(
        v_h.at[:, :, pl.ds(pl.multiple_of(seat * part, L), part)], vparts.at[seat], load_sem.at[2]
    )
    near_load.start()
    u_load.start()
    v_load.start()

    spread = (iota((YC, W), 0) == lax.div(iota((YC, W), 1), E)).astype(F32)

    def first(x, c):
        wide = lax.dot_general(
            coef[x], spread, (((0,), (0,)), ((), ())),
            precision=HIGHEST, preferred_element_type=F32,
        )
        r = 1.0 / (6.0 + wide)
        rinv[x] = r
        u1[x + 1] = src[x] * r
        return c

    for load in loads:
        load.wait()
    lax.fori_loop(0, CX, first, 0)

    rows8 = iota((CX, W), 0)

    def plane(ref, off, depth):
        out = jnp.zeros((CX, W), F32)
        for x in range(CX):
            row = jnp.where(
                gz == 0,
                ref[x + off, depth : depth + 1, :],
                ref[x + off, DZ - 1 - depth : DZ - depth, :],
            )
            out = jnp.where(rows8 == x, row, out)
        return out

    for n, (ref, off, depth) in enumerate(
        ((src, 0, 0), (rinv, 0, 0), (u1, 1, 1), (u1, 1, 0), (src, 0, 1), (rinv, 0, 1), (u1, 1, 2))
    ):
        planes[n] = plane(ref, off, depth)
    for side, (edge, inner, lane) in enumerate(((0, 1, 0), (CX - 1, CX - 2, W - L))):
        for n in range(3):
            xs[side, n : n + 1, :] = planes[n, edge : edge + 1, :]
        xs[side, 3:4, :] = planes[3, inner : inner + 1, :]
        for n in range(4):
            ys[side, n] = planes[n, :, lane : lane + L]
        for b, lane_b in enumerate((0, W - L)):
            cs[2 * side + b] = planes[3, edge : edge + 1, lane_b : lane_b + L]

    lanes_col = iota((8, L), 1)
    row = jnp.where(lanes_col == 0, ncol[0, 0, 0], 0)
    for k in range(far):
        row = jnp.where(lanes_col == k + 1, fcol[0, 0, 0, k], row)
    cols_v[seat] = row

    lanes32 = lax.div(iota((DZ, L), 1), E)

    def pack(u, n):
        if n > 0:
            for side, x in enumerate((1, CX)):
                edge = u[x] if n == 1 else u[x] - u1[x]
                vxs[n - 1, side] = edge.astype(BF16)

        def step(k, c):
            low = jnp.zeros((DZ, L), F32)
            high = jnp.zeros((DZ, L), F32)
            for j in range(4):
                cell = u[4 * k + j + 1]
                low = jnp.where(lanes32 == j, pltpu.roll(cell[:, :L], E * j, 1), low)
                high = jnp.where(
                    lanes32 == j, pltpu.roll(cell[:, W - L :], (E * j - (L - E)) % L, 1), high
                )
            vys[n, 0, k] = low
            vys[n, 1, k] = high
            return c

        lax.fori_loop(0, CX // 4, step, 0)

        def zstep(x, c):
            vzs[n, x] = jnp.where(gz == 0, u[x + 1, DZ - 1 : DZ, :], u[x + 1, 0:1, :])
            return c

        lax.fori_loop(0, CX, zstep, 0)

    pack(u1, 0)

    for side, have in ((0, low_x), (1, high_x)):

        @pl.when(jnp.logical_not(have))
        def _(side=side):
            xr[side] = jnp.zeros((4, W), F32)
            for u in (u1, u2, u3):
                u[side * (CX + 1)] = jnp.zeros((DZ, W), F32)

    for side, have in ((0, low_y), (1, high_y)):

        @pl.when(jnp.logical_not(have))
        def _(side=side):
            yr[side] = jnp.zeros((4, CX, L), F32)
            for n in range(3):
                vyr[n, side] = jnp.zeros((CX // 4, DZ, L), F32)

    for a, hx in ((0, low_x), (1, high_x)):
        for b, hy in ((0, low_y), (1, high_y)):

            @pl.when(jnp.logical_not(jnp.logical_and(hx, hy)))
            def _(a=a, b=b):
                cr[2 * a + b] = jnp.zeros((1, L), F32)

    pl.semaphore_wait(bar, count)

    sides = ((0, low_x, -1), (1, high_x, 1))
    sides_y = ((0, low_y, -1), (1, high_y, 1))

    def x_copy(side, dx):
        return remote(xs.at[side], xr.at[1 - side], x_ss.at[side], x_rs.at[1 - side], (gx + dx, gy, gz))

    def y_copy(side, dy):
        return remote(
            ys.at[side], yr.at[1 - side], x_ss.at[2 + side], x_rs.at[3 - side], (gx, gy + dy, gz)
        )

    def c_copy(a, dx, b, dy):
        there = 2 * (1 - a) + 1 - b
        return remote(
            cs.at[2 * a + b], cr.at[there], c_ss.at[2 * a + b], c_rs.at[there], (gx + dx, gy + dy, gz)
        )

    def x_halo(act):
        for side, have, dx in sides:

            @pl.when(have)
            def _(side=side, dx=dx):
                act(x_copy(side, dx), 0)

    def c_halo(act):
        for a, hx, dx in sides:
            for b, hy, dy in sides_y:

                @pl.when(jnp.logical_and(hx, hy))
                def _(a=a, dx=dx, b=b, dy=dy):
                    act(c_copy(a, dx, b, dy), 0)

    def y_halo(act):
        for side, have, dy in sides_y:

            @pl.when(have)
            def _(side=side, dy=dy):
                act(y_copy(side, dy), 0)

    def narrow_recv():
        for side, have, dx in sides:

            @pl.when(have)
            def _(side=side, dx=dx):
                remote(
                    xs.at[side], xr.at[side], x_ss.at[side], x_rs.at[side], (gx + dx, gy, gz)
                ).wait_recv()

        for side, have, dy in sides_y:

            @pl.when(have)
            def _(side=side, dy=dy):
                remote(
                    ys.at[side], yr.at[side], x_ss.at[2 + side], x_rs.at[2 + side], (gx, gy + dy, gz)
                ).wait_recv()

        for a, hx, dx in sides:
            for b, hy, dy in sides_y:

                @pl.when(jnp.logical_and(hx, hy))
                def _(a=a, dx=dx, b=b, dy=dy):
                    remote(
                        cs.at[2 * a + b], cr.at[2 * a + b], c_ss.at[2 * a + b], c_rs.at[2 * a + b],
                        (gx + dx, gy + dy, gz),
                    ).wait_recv()

    def start(copy, _):
        copy.start()

    def sent(copy, _):
        copy.wait_send()

    x_halo(start)
    c_halo(start)
    y_halo(start)

    def ft_copy():
        return remote(ft, ftr, ft_sem.at[0], ft_sem.at[1], (anti, gy, gz))

    ft_copy().start()

    def peer(d):
        return lax.rem(gy + d, n_gy)

    def source_of(d):
        return lax.rem(gy + n_gy - d, n_gy)

    def mate(d):
        return lax.rem(seat + d, team)

    def mate_from(d):
        return lax.rem(seat + team - d, team)

    def col_send(d):
        return remote(
            cols_v.at[seat], cols_v.at[seat], col_ss.at[d], col_rs.at[d], (gx, bench + mate(d), gz)
        )

    def col_recv(d):
        s = mate_from(d)
        return remote(cols_v.at[s], cols_v.at[s], col_ss.at[d], col_rs.at[d], (gx, bench + s, gz))

    def vp_send(d):
        t = mate(d)
        return remote(
            v_h.at[:, :, pl.ds(pl.multiple_of(t * part, L), part)], vparts.at[seat],
            vp_ss.at[d], vp_rs.at[d], (gx, bench + t, gz),
        )

    def vp_recv(d):
        s = mate_from(d)
        return remote(vparts.at[s], vparts.at[s], vp_ss.at[d], vp_rs.at[d], (gx, bench + s, gz))

    def each(n, f):
        def step(d, c):
            f(d)
            return c

        lax.fori_loop(1, n, step, 0)

    each(team, lambda d: col_send(d).start())

    fields = (u1, u2, u3)

    def vol_send(n, act):
        u = fields[n]
        for side, have, dx in sides:

            @pl.when(have)
            def _(side=side, dx=dx):
                out = vxs.at[n - 1, side] if n > 0 else u.at[1 + side * (CX - 1)]
                there = vxr.at[n - 1, 1 - side] if n > 0 else u.at[(1 - side) * (CX + 1)]
                act(
                    remote(
                        out, there,
                        v_ss.at[n, side], v_rs.at[n, 1 - side], (gx + dx, gy, gz),
                    ),
                    0,
                )

        for side, have, dy in sides_y:

            @pl.when(have)
            def _(side=side, dy=dy):
                act(
                    remote(
                        vys.at[n, side], vyr.at[n, 1 - side],
                        v_ss.at[n, 2 + side], v_rs.at[n, 3 - side], (gx, gy + dy, gz),
                    ),
                    0,
                )

        act(remote(vzs.at[n], vzr.at[n], v_ss.at[n, 4], v_rs.at[n, 4], (gx, gy, other)), 0)

    def vol_recv(n):
        u = fields[n]
        for side, have, dx in sides:

            @pl.when(have)
            def _(side=side, dx=dx):
                halo = vxr.at[n - 1, side] if n > 0 else u.at[side * (CX + 1)]
                remote(halo, halo, v_ss.at[n, side], v_rs.at[n, side], (gx + dx, gy, gz)).wait_recv()
                if n > 0:
                    edge = vxr[n - 1, side].astype(F32)
                    x = side * (CX + 1)
                    u[x] = edge if n == 1 else edge + u1[x]

        for side, have, dy in sides_y:

            @pl.when(have)
            def _(side=side, dy=dy):
                halo = vyr.at[n, side]
                remote(
                    halo, halo, v_ss.at[n, 2 + side], v_rs.at[n, 2 + side], (gx, gy + dy, gz)
                ).wait_recv()

        remote(vzr.at[n], vzr.at[n], v_ss.at[n, 4], v_rs.at[n, 4], (gx, gy, other)).wait_recv()

    vol_send(0, start)

    def tables(table, slot):
        spot = iota((part, total_y), 0) + seat * part
        col = iota((part, total_y), 1)
        cell = jnp.zeros((part, total_y), I32)
        for x in range(CX):
            cell = jnp.where(table[x] == spot, col + x * total_y, cell)
        cell = jnp.sum(cell.astype(F32), axis=1, keepdims=True).astype(I32)
        x = lax.div(cell, total_y)
        y = cell - x * total_y
        y8 = lax.div(y, 8)
        pick[slot] = (iota((part, 16 * n_gy), 1) == y8 * 8 + x).astype(BF16)
        mask[slot] = (lax.div(iota((part, 256), 1), E) == y - y8 * 8).astype(BF16)

    tables(ft, 0)
    spots = iota((tile, L), 0)
    for j in range(n_gy):
        line = jnp.concatenate([ft[x][:, YC * j : YC * (j + 1)] for x in range(CX)], axis=1)
        onehot[:, L * j : L * (j + 1)] = (spots == line).astype(F32).astype(BF16)

    narrow_recv()
    s0, r0, a1, a0 = planes[0], planes[1], planes[2], planes[3]
    s1, r1, a2 = planes[4], planes[5], planes[6]
    lo, hi = yr[0], yr[1]

    def bc(v, n=W):
        return jnp.broadcast_to(v, (CX, n))

    def left(v):
        return pltpu.roll(v, E, 1)

    def right(v):
        return pltpu.roll(v, L - E, 1)

    cor = [[cr[0], cr[1]], [cr[2], cr[3]]]
    edge_u1 = []
    edge_u2 = []
    edge_b1 = []
    for side in range(2):
        hs, hr, h1, h2 = (bc(xr[side, n : n + 1, :]) for n in range(4))
        hu = hs * hr
        at = bc(a0[(CX - 1) * side : (CX - 1) * side + 1, :])
        beside = along_y(hu, left(bc(cor[side][0], L)), right(bc(cor[side][1], L)))
        edge_u1.append(hu)
        edge_b1.append(h1)
        edge_u2.append((hs + h2 + at + h1 + beside) * hr)
    lu2 = lo[0] + left(lo[3]) + right(a0[:, :L]) + lo[2]
    lu2 = (lu2 + along_x(lo[3], bc(cor[0][0], L), bc(cor[1][0], L))) * lo[1]
    hu2 = hi[0] + right(hi[3]) + left(a0[:, W - L :]) + hi[2]
    hu2 = (hu2 + along_x(hi[3], bc(cor[0][1], L), bc(cor[1][1], L))) * hi[1]
    b0 = (s0 + a1 + along_x(a0, edge_u1[0], edge_u1[1]) + along_y(a0, left(lo[3]), right(hi[3]))) * r0
    b1 = (
        s1 + a0 + a2 + along_x(a1, edge_b1[0], edge_b1[1]) + along_y(a1, left(lo[2]), right(hi[2]))
    ) * r1
    face = (s0 + b1 + along_x(b0, edge_u2[0], edge_u2[1]) + along_y(b0, left(lu2), right(hu2))) * r0
    faces[zh, gy] = jnp.concatenate([face[:, : W // 2], face[:, W // 2 :]], axis=0).astype(BF16)

    def ring_d(k):
        half = lax.div(k, 2)
        return n_gy + half * (1 - 2 * lax.rem(k, 2))

    def f_send(k):
        d = ring_d(k)
        bz, by = ring_pos(d)
        return remote(
            faces.at[zh, gy], faces.at[zh, gy], f_ss.at[d], f_rs.at[d], (2 * q + bz, by, gz)
        )

    def f_recv(k):
        d = ring_d(k)
        bz, by = ring_pos(ring - d)
        return remote(
            faces.at[bz, by], faces.at[bz, by], f_ss.at[d], f_rs.at[d], (2 * q + bz, by, gz)
        )

    each(ring, lambda k: f_send(k).start())

    each(team, lambda d: vp_send(d).start())

    remote(ft, ftr, ft_sem.at[0], ft_sem.at[1], (anti, gy, gz)).wait_recv()
    tables(ftr, 1)
    u_load.wait()
    flat = far * rank
    u_v_all = u_v[...]
    u_p[:flat, :] = dot_nn(u_v_all, onehot[...]).astype(BF16)
    u_p[flat:, :] = jnp.zeros((L - flat, tile), BF16)
    near_load.wait()
    chunk = min(256, tile)
    for n in range(tile // chunk):
        near_p[n * chunk : (n + 1) * chunk, :] = dot_tn(
            near_v[:, n * chunk : (n + 1) * chunk], onehot[...]
        ).astype(BF16)

    rows32 = iota((DZ, W), 0)
    lanes128 = iota((DZ, L), 1)

    def sweep(n, store):
        u = fields[n]

        def step(k, c):
            for j in range(4):
                x = 4 * k + j
                cell = u[x + 1]
                zrow = vzr[n, x]
                up = jnp.where(rows32 == DZ - 1, jnp.where(gz == 0, zrow, 0.0), pltpu.roll(cell, DZ - 1, 0))
                down = jnp.where(rows32 == 0, jnp.where(gz == 0, 0.0, zrow), pltpu.roll(cell, 1, 0))
                low = pltpu.roll(vyr[n, 0, k], (L - E * j) % L, 1)
                high = pltpu.roll(vyr[n, 1, k], (L - E - E * j) % L, 1)
                total = src[x] + u[x] + u[x + 2] + up + down + along_y(cell, low, high)
                store(x, total)
            return c

        lax.fori_loop(0, CX // 4, step, 0)

    def keep(u):
        def store(x, total):
            u[x + 1] = total * rinv[x]

        return store

    each(team, lambda d: col_recv(d).wait_recv())
    to_smem = pltpu.make_async_copy(cols_v, cols_s, smem_sem)
    to_smem.start()
    to_smem.wait()

    each(ring, lambda k: f_recv(k).wait_recv())

    fold = (lax.rem(iota((E, 256), 1), E) == iota((E, 256), 0)).astype(BF16)
    for slot, (half, block) in enumerate(((zh, gx), (1 - zh, anti))):
        flat_faces = faces[half].reshape(16 * n_gy, 256)
        picked = dot_nn(pick[slot], flat_faces).astype(BF16) * mask[slot]
        gath[gz * n_gx + block] = dot_nt(fold, picked).astype(BF16)

    def mine(qq, side):
        return gath.at[pl.ds(side * n_gx + 2 * qq, 2)]

    def g_send(d):
        t = lax.rem(q + d, nq)
        return remote(mine(q, gz), mine(q, gz), g_ss.at[d], g_rs.at[d], (2 * t + zh, gy, gz))

    def g_recv(d):
        s = lax.rem(q + nq - d, nq)
        return remote(mine(s, gz), mine(s, gz), g_ss.at[d], g_rs.at[d], (2 * s + zh, gy, gz))

    def k_send(d):
        s = lax.rem(q + nq - d, nq)
        return remote(mine(s, gz), mine(s, gz), k_ss.at[d], k_rs.at[d], (gx, gy, other))

    def k_recv(d):
        s = lax.rem(q + nq - d, nq)
        return remote(mine(s, other), mine(s, other), k_ss.at[d], k_rs.at[d], (gx, gy, other))

    each(nq, lambda d: g_send(d).start())
    k_send(0).start()

    vol_recv(0)
    sweep(0, keep(u2))
    pack(u2, 1)
    vol_send(1, start)

    v_load.wait()
    each(team, lambda d: vp_recv(d).wait_recv())
    group = lax.div(iota((flat, part), 0), rank)

    def blocks(j, c):
        parts = vparts[j].reshape(flat, part)
        for k in range(far):
            vblk[j, :flat, k * part : (k + 1) * part] = jnp.where(group == k, parts, jnp.zeros_like(parts))
        if flat < L:
            vblk[j, flat:, :] = jnp.zeros((L - flat, far * part), BF16)
        return c

    lax.fori_loop(0, team, blocks, 0)

    def forward(d):
        g_recv(d).wait_recv()
        k_send(d).start()

    each(nq, forward)
    k_recv(0).wait_recv()
    each(nq, lambda d: k_recv(d).wait_recv())

    def w_send(d):
        t = mate(d)
        return remote(ws.at[t], wr.at[seat], w_ss.at[d], w_rs.at[d], (gx, bench + t, gz))

    def w_recv(d):
        s = mate_from(d)
        return remote(wr.at[s], wr.at[s], w_ss.at[d], w_rs.at[d], (gx, bench + s, gz))

    def n_send(d):
        t = mate(d)
        return remote(ns.at[t], nr.at[seat], n_ss.at[d], n_rs.at[d], (gx, bench + t, gz))

    def n_recv(d):
        s = mate_from(d)
        return remote(nr.at[s], nr.at[s], n_ss.at[d], n_rs.at[d], (gx, bench + s, gz))

    def column(j, k):
        c = cols_s[j, 0, k]
        return gath[lax.rem(c, 2) * n_gx + lax.div(c, 2)]

    def partial_weights(t):
        for k in range(far):
            tsel[:, k * part : (k + 1) * part] = column(t, k + 1)
        return dot_nt(tsel[...], vblk[t])

    def near_out(d):
        t = mate(d)
        ns[t] = column(t, 0)
        n_send(d).start()

    each(team, near_out)
    nr[seat] = column(seat, 0)

    def weights_out(d):
        t = mate(d)
        ws[t] = partial_weights(t)
        w_send(d).start()

    each(team, weights_out)
    wr[seat] = partial_weights(seat)

    vol_recv(1)
    sweep(1, keep(u3))
    pack(u3, 2)
    vol_send(2, start)

    each(team, lambda d: n_recv(d).wait_recv())
    near_t = jnp.concatenate([nr[j] for j in range(team)], axis=1)
    acc = dot_nn(near_t, near_p[...])
    each(team, lambda d: w_recv(d).wait_recv())
    weights = wr[0]
    for j in range(1, team):
        weights = weights + wr[j]
    acc = acc + dot_nn(weights.astype(BF16), u_p[...])
    for j in range(n_gy):
        rs[j] = acc[:, j * L : (j + 1) * L]

    def r_send(d):
        t = peer(d)
        return remote(rs.at[t], rr.at[gy], r_ss.at[d], r_rs.at[d], (gx, t, gz))

    def r_recv(d):
        s = source_of(d)
        return remote(rr.at[s], rr.at[s], r_ss.at[d], r_rs.at[d], (gx, s, gz))

    each(n_gy, lambda d: r_send(d).start())
    rr[gy] = rs[gy]

    def hold(x, total):
        sol[x] = total

    x_halo(sent)
    c_halo(sent)
    y_halo(sent)
    ft_copy().wait_send()
    each(team, lambda d: col_send(d).wait_send())
    each(team, lambda d: vp_send(d).wait_send())
    each(ring, lambda k: f_send(k).wait_send())
    each(nq, lambda d: g_send(d).wait_send())
    k_send(0).wait_send()
    each(nq, lambda d: k_send(d).wait_send())
    each(team, lambda d: n_send(d).wait_send())
    each(team, lambda d: w_send(d).wait_send())
    for n in range(3):
        vol_send(n, sent)
    vol_recv(2)
    sweep(2, hold)
    each(n_gy, lambda d: r_recv(d).wait_recv())
    total = rr[0]
    for j in range(1, n_gy):
        total = total + rr[j]
    widen = (iota((E, W), 0) == lax.rem(iota((E, W), 1), E)).astype(F32)
    wide = jnp.dot(total.T, widen, precision=HIGHEST, preferred_element_type=F32)
    keep_cell = lax.rem(iota((L, W), 0), YC) == lax.div(iota((L, W), 1), E)
    value = jnp.sum(jnp.where(keep_cell, wide, 0.0).reshape(CX, YC, W), axis=1)
    face_z = (DZ - 1) * gz
    for x in range(CX):
        line = value[x : x + 1, :]
        flux[x] = line
        sol[x] = (sol[x] + jnp.where(rows32 == face_z, line, 0.0)) * rinv[x]

    each(n_gy, lambda d: r_send(d).wait_send())


def body(source, coef, face_trace, near_col, far_col, near_tile, far_u, far_v):
    n_gx = lax.axis_size("gx")
    n_gy = lax.axis_size("gy")
    far, rank, tile = far_u.shape[3:]
    total_y = face_trace.shape[2]
    nq, ring, flat = n_gx // 2, 2 * n_gy, far * rank
    team = min(TEAM, n_gy)
    part = tile // team
    cfg = (n_gx, n_gy, far, rank, total_y)
    vmem = pl.BlockSpec(memory_space=pltpu.VMEM)
    anyspace = pl.BlockSpec(memory_space=pl.ANY)
    dma = pltpu.SemaphoreType.DMA
    scratch = [
        pltpu.SMEM((1, 1, 1), I32),
        pltpu.SMEM((1, 1, 1, far), I32),
        pltpu.VMEM((CX, DZ, W), F32),
        pltpu.VMEM((CX, YC, DZ), F32),
        pltpu.VMEM((CX, 1, total_y), I32),
        pltpu.VMEM((CX + 2, DZ, W), F32),
        pltpu.VMEM((CX + 2, DZ, W), F32),
        pltpu.VMEM((CX + 2, DZ, W), F32),
        pltpu.VMEM((CX, DZ, W), F32),
        pltpu.VMEM((7, CX, W), F32),
        pltpu.VMEM((2, 4, W), F32),
        pltpu.VMEM((2, 4, W), F32),
        pltpu.VMEM((2, 4, CX, L), F32),
        pltpu.VMEM((2, 4, CX, L), F32),
        pltpu.VMEM((4, 1, L), F32),
        pltpu.VMEM((4, 1, L), F32),
        pltpu.VMEM((2, 2, DZ, W), BF16),
        pltpu.VMEM((2, 2, DZ, W), BF16),
        pltpu.VMEM((3, 2, CX // 4, DZ, L), F32),
        pltpu.VMEM((3, 2, CX // 4, DZ, L), F32),
        pltpu.VMEM((3, CX, 1, W), F32),
        pltpu.VMEM((3, CX, 1, W), F32),
        pltpu.VMEM((CX, 1, total_y), I32),
        pltpu.VMEM((team, 8, L), I32),
        pltpu.SMEM((team, 8, L), I32),
        pltpu.VMEM((2, part, 16 * n_gy), BF16),
        pltpu.VMEM((2, part, 256), BF16),
        pltpu.VMEM((2, n_gy, 16, 256), BF16),
        pltpu.VMEM((2 * n_gx, E, part), BF16),
        pltpu.VMEM((tile, tile), BF16),
        pltpu.VMEM((tile, tile), BF16),
        pltpu.VMEM((tile, tile), BF16),
        pltpu.VMEM((flat, tile), BF16),
        pltpu.VMEM((L, tile), BF16),
        pltpu.VMEM((team, far, rank, part), BF16),
        pltpu.VMEM((team, L, far * part), BF16),
        pltpu.VMEM((E, far * part), BF16),
        pltpu.VMEM((team, E, part), BF16),
        pltpu.VMEM((team, E, part), BF16),
        pltpu.VMEM((team, E, L), F32),
        pltpu.VMEM((team, E, L), F32),
        pltpu.VMEM((n_gy, E, L), F32),
        pltpu.VMEM((n_gy, E, L), F32),
        dma((3,)),
        dma((5,)),
        dma((4,)), dma((4,)),
        dma((4,)), dma((4,)),
        dma((3, 5)), dma((3, 5)),
        dma((2,)),
        dma((n_gy,)), dma((n_gy,)),
        dma,
        dma((ring,)), dma((ring,)),
        dma((nq,)), dma((nq,)),
        dma((nq,)), dma((nq,)),
        dma((n_gy,)), dma((n_gy,)),
        dma((n_gy,)), dma((n_gy,)),
        dma((n_gy,)), dma((n_gy,)),
        dma((n_gy,)), dma((n_gy,)),
    ]
    return pl.pallas_call(
        functools.partial(kernel, cfg),
        out_shape=(
            jax.ShapeDtypeStruct(source.shape, F32),
            jax.ShapeDtypeStruct((CX, 1, W), F32),
        ),
        in_specs=[anyspace] * 8,
        out_specs=(vmem, vmem),
        scratch_shapes=scratch,
        compiler_params=pltpu.CompilerParams(
            collective_id=0, has_side_effects=True, vmem_limit_bytes=60 * 1024 * 1024
        ),
        name="coupled_step",
    )(
        near_col,
        far_col,
        source,
        coef.swapaxes(1, 2),
        face_trace,
        near_tile.reshape(tile, tile),
        far_u.reshape(flat, tile),
        far_v.reshape(far, rank, tile),
    )


def solution(mesh):
    return jax.shard_map(
        body,
        mesh=mesh,
        in_specs=(
            P("gx", "gz", "gy"),
            P("gx", "gz", "gy"),
            P("gx", "gz", None),
            P("gx", "gz", "gy"),
            P("gx", "gz", "gy", None),
            P("gx", "gz", "gy", None, None),
            P("gx", "gz", "gy", None, None, None),
            P("gx", "gz", "gy", None, None, None),
        ),
        out_specs=(P("gx", "gz", "gy"), P("gx", "gz", "gy")),
        check_vma=False,
    )
```

```python
import functools

import jax
import jax.numpy as jnp
from jax import lax
from jax.experimental import pallas as pl
from jax.experimental.pallas import tpu as pltpu
from jax.sharding import PartitionSpec as P

E = 32
CX = 8
YC = 16
DZ = 32
W = YC * E
L = 128
F32 = jnp.float32
BF16 = jnp.bfloat16
I32 = jnp.int32
TEAM = 4
MESH = pl.DeviceIdType.MESH
HIGHEST = lax.Precision.HIGHEST


def dot_nt(a, b):
    return lax.dot_general(a, b, (((1,), (1,)), ((), ())), preferred_element_type=F32)


def dot_tn(a, b):
    return lax.dot_general(a, b, (((0,), (0,)), ((), ())), preferred_element_type=F32)


def dot_nn(a, b):
    return lax.dot_general(a, b, (((1,), (0,)), ((), ())), preferred_element_type=F32)


def iota(shape, dim):
    return lax.broadcasted_iota(I32, shape, dim)


def along_x(field, low, high):
    rows = iota(field.shape, 0)
    before = jnp.where(rows == 0, low, pltpu.roll(field, 1, 0))
    after = jnp.where(rows == field.shape[0] - 1, high, pltpu.roll(field, field.shape[0] - 1, 0))
    return before + after


def along_y(field, low, high):
    n = field.shape[0]
    lanes = iota((n, L), 1)
    before = pltpu.roll(field, E, 1)
    after = pltpu.roll(field, W - E, 1)
    first = jnp.where(lanes < E, low, before[:, :L])
    last = jnp.where(lanes >= L - E, high, after[:, W - L :])
    before = jnp.concatenate([first, before[:, L:]], axis=1)
    after = jnp.concatenate([after[:, : W - L], last], axis=1)
    return before + after


def kernel(
    cfg,
    ncol_h, fcol_h, src_h, coef_h, ft_h, near_h, u_h, v_h,
    sol, flux,
    ncol, fcol, src, coef, ft,
    u1, u2, u3, rinv, planes,
    xs, xr, ys, yr, cs, cr,
    vxs, vxr, vys, vyr, vzs, vzr,
    ftr, cols_v, cols_s,
    pick, mask, faces, gath,
    near_v, near_p, onehot, u_v, u_p,
    vparts, vblk, tsel, ns, nr, ws, wr, rs, rr, rsb, rrb,
    load_sem, in_sem, x_ss, x_rs, c_ss, c_rs, v_ss, v_rs, vx_ss, vx_rs, ft_sem, col_ss, col_rs, smem_sem,
    f_ss, f_rs, g_ss, g_rs, k_ss, k_rs, vp_ss, vp_rs, n_ss, n_rs, w_ss, w_rs, r_ss, r_rs, b_ss, b_rs,
):
    n_gx, n_gy, far, rank, total_y = cfg
    tile = CX * total_y
    team = min(TEAM, n_gy)
    part = tile // team
    nq = n_gx // 2
    ring = 2 * n_gy
    gx = lax.axis_index("gx")
    gy = lax.axis_index("gy")
    gz = lax.axis_index("gz")
    zh = lax.rem(gx, 2)
    q = lax.div(gx, 2)
    anti = gx + 1 - 2 * zh
    other = 1 - gz
    me = zh * n_gy + gy
    seat = lax.rem(gy, team)
    bench = gy - seat
    low_x, high_x = gx > 0, gx < n_gx - 1
    low_y, high_y = gy > 0, gy < n_gy - 1

    def remote(a, b, ssem, rsem, dev):
        return pltpu.make_async_remote_copy(
            src_ref=a, dst_ref=b, send_sem=ssem, recv_sem=rsem, device_id=dev, device_id_type=MESH
        )

    bar = pltpu.get_barrier_semaphore()

    def signal(x, y, z):
        pl.semaphore_signal(bar, inc=1, device_id=(x, y, z), device_id_type=MESH)

    count = ring - 1 + nq - 1 + 1
    for dx, hx in ((-1, low_x), (1, high_x)):
        for dy, hy in ((-1, low_y), (0, None), (1, high_y)):
            cond = hx if hy is None else jnp.logical_and(hx, hy)
            count = count + cond.astype(I32)

            @pl.when(cond)
            def _(dx=dx, dy=dy):
                signal(gx + dx, gy + dy, gz)

    def ring_pos(d):
        pos = lax.rem(me + d, ring)
        return lax.div(pos, n_gy), lax.rem(pos, n_gy)

    def ring_signal(d, c):
        bz, by = ring_pos(d)
        signal(2 * q + bz, by, gz)
        return c

    lax.fori_loop(1, ring, ring_signal, 0)

    def xy_signal(d, c):
        signal(2 * lax.rem(q + d, nq) + zh, gy, gz)
        return c

    lax.fori_loop(1, nq, xy_signal, 0)
    signal(gx, gy, other)

    loads = [
        pltpu.make_async_copy(a, b, in_sem.at[n])
        for n, (a, b) in enumerate(
            ((coef_h, coef), (src_h, src), (ft_h, ft), (ncol_h, ncol), (fcol_h, fcol))
        )
    ]
    for load in loads:
        load.start()
    near_load = pltpu.make_async_copy(near_h, near_v, load_sem.at[0])
    u_load = pltpu.make_async_copy(u_h, u_v, load_sem.at[1])
    v_load = pltpu.make_async_copy(
        v_h.at[:, :, pl.ds(pl.multiple_of(seat * part, L), part)], vparts.at[seat], load_sem.at[2]
    )
    near_load.start()
    u_load.start()
    v_load.start()

    spread = (iota((YC, W), 0) == lax.div(iota((YC, W), 1), E)).astype(F32)

    def first(x, c):
        wide = lax.dot_general(
            coef[x], spread, (((0,), (0,)), ((), ())),
            precision=HIGHEST, preferred_element_type=F32,
        )
        r = 1.0 / (6.0 + wide)
        rinv[x] = r
        u1[x + 1] = src[x] * r
        return c

    for load in loads:
        load.wait()
    lax.fori_loop(0, CX, first, 0)

    rows8 = iota((CX, W), 0)

    def plane(ref, off, depth):
        out = jnp.zeros((CX, W), F32)
        for x in range(CX):
            row = jnp.where(
                gz == 0,
                ref[x + off, depth : depth + 1, :],
                ref[x + off, DZ - 1 - depth : DZ - depth, :],
            )
            out = jnp.where(rows8 == x, row, out)
        return out

    for n, (ref, off, depth) in enumerate(
        ((src, 0, 0), (rinv, 0, 0), (u1, 1, 1), (u1, 1, 0), (src, 0, 1), (rinv, 0, 1), (u1, 1, 2))
    ):
        planes[n] = plane(ref, off, depth)
    for side, (edge, inner, lane) in enumerate(((0, 1, 0), (CX - 1, CX - 2, W - L))):
        for n in range(3):
            xs[side, n : n + 1, :] = planes[n, edge : edge + 1, :]
        xs[side, 3:4, :] = planes[3, inner : inner + 1, :]
        for n in range(4):
            ys[side, n] = planes[n, :, lane : lane + L]
        for b, lane_b in enumerate((0, W - L)):
            cs[2 * side + b] = planes[3, edge : edge + 1, lane_b : lane_b + L]

    lanes_col = iota((8, L), 1)
    row = jnp.where(lanes_col == 0, ncol[0, 0, 0], 0)
    for k in range(far):
        row = jnp.where(lanes_col == k + 1, fcol[0, 0, 0, k], row)
    cols_v[seat] = row

    lanes32 = lax.div(iota((DZ, L), 1), E)

    def pack_x(slot):
        for side, x in enumerate((1, CX)):
            if slot == 0:
                coarse = u1[x].astype(BF16)
                vxs[0, side] = coarse
                vxs[1, side] = (u1[x] - coarse.astype(F32)).astype(BF16)
            elif slot == 2:
                vxs[2, side] = u2[x].astype(BF16)
            else:
                vxs[3, side] = (u3[x] - u1[x]).astype(BF16)

    def pack(u, n):
        def step(k, c):
            low = jnp.zeros((DZ, L), F32)
            high = jnp.zeros((DZ, L), F32)
            for j in range(4):
                cell = u[4 * k + j + 1]
                low = jnp.where(lanes32 == j, pltpu.roll(cell[:, :L], E * j, 1), low)
                high = jnp.where(
                    lanes32 == j, pltpu.roll(cell[:, W - L :], (E * j - (L - E)) % L, 1), high
                )
            vys[n, 0, k] = low
            vys[n, 1, k] = high
            return c

        lax.fori_loop(0, CX // 4, step, 0)

        def zstep(x, c):
            vzs[n, x] = jnp.where(gz == 0, u[x + 1, DZ - 1 : DZ, :], u[x + 1, 0:1, :])
            return c

        lax.fori_loop(0, CX, zstep, 0)

    pack_x(0)
    pack(u1, 0)

    for side, have in ((0, low_x), (1, high_x)):

        @pl.when(jnp.logical_not(have))
        def _(side=side):
            xr[side] = jnp.zeros((4, W), F32)
            for u in (u1, u2, u3):
                u[side * (CX + 1)] = jnp.zeros((DZ, W), F32)

    for side, have in ((0, low_y), (1, high_y)):

        @pl.when(jnp.logical_not(have))
        def _(side=side):
            yr[side] = jnp.zeros((4, CX, L), F32)
            for n in range(3):
                vyr[n, side] = jnp.zeros((CX // 4, DZ, L), F32)

    for a, hx in ((0, low_x), (1, high_x)):
        for b, hy in ((0, low_y), (1, high_y)):

            @pl.when(jnp.logical_not(jnp.logical_and(hx, hy)))
            def _(a=a, b=b):
                cr[2 * a + b] = jnp.zeros((1, L), F32)

    pl.semaphore_wait(bar, count)

    sides = ((0, low_x, -1), (1, high_x, 1))
    sides_y = ((0, low_y, -1), (1, high_y, 1))

    def x_copy(side, dx):
        return remote(xs.at[side], xr.at[1 - side], x_ss.at[side], x_rs.at[1 - side], (gx + dx, gy, gz))

    def y_copy(side, dy):
        return remote(
            ys.at[side], yr.at[1 - side], x_ss.at[2 + side], x_rs.at[3 - side], (gx, gy + dy, gz)
        )

    def c_copy(a, dx, b, dy):
        there = 2 * (1 - a) + 1 - b
        return remote(
            cs.at[2 * a + b], cr.at[there], c_ss.at[2 * a + b], c_rs.at[there], (gx + dx, gy + dy, gz)
        )

    def x_halo(act):
        for side, have, dx in sides:

            @pl.when(have)
            def _(side=side, dx=dx):
                act(x_copy(side, dx), 0)

    def c_halo(act):
        for a, hx, dx in sides:
            for b, hy, dy in sides_y:

                @pl.when(jnp.logical_and(hx, hy))
                def _(a=a, dx=dx, b=b, dy=dy):
                    act(c_copy(a, dx, b, dy), 0)

    def y_halo(act):
        for side, have, dy in sides_y:

            @pl.when(have)
            def _(side=side, dy=dy):
                act(y_copy(side, dy), 0)

    def narrow_recv():
        for side, have, dx in sides:

            @pl.when(have)
            def _(side=side, dx=dx):
                remote(
                    xs.at[side], xr.at[side], x_ss.at[side], x_rs.at[side], (gx + dx, gy, gz)
                ).wait_recv()

        for side, have, dy in sides_y:

            @pl.when(have)
            def _(side=side, dy=dy):
                remote(
                    ys.at[side], yr.at[side], x_ss.at[2 + side], x_rs.at[2 + side], (gx, gy + dy, gz)
                ).wait_recv()

        for a, hx, dx in sides:
            for b, hy, dy in sides_y:

                @pl.when(jnp.logical_and(hx, hy))
                def _(a=a, dx=dx, b=b, dy=dy):
                    remote(
                        cs.at[2 * a + b], cr.at[2 * a + b], c_ss.at[2 * a + b], c_rs.at[2 * a + b],
                        (gx + dx, gy + dy, gz),
                    ).wait_recv()

    def start(copy, _):
        copy.start()

    def sent(copy, _):
        copy.wait_send()

    x_halo(start)
    c_halo(start)
    y_halo(start)

    def ft_copy():
        return remote(ft, ftr, ft_sem.at[0], ft_sem.at[1], (anti, gy, gz))

    ft_copy().start()

    def peer(d):
        return lax.rem(gy + d, n_gy)

    def source_of(d):
        return lax.rem(gy + n_gy - d, n_gy)

    def mate(d):
        return lax.rem(seat + d, team)

    def mate_from(d):
        return lax.rem(seat + team - d, team)

    def col_send(d):
        return remote(
            cols_v.at[seat], cols_v.at[seat], col_ss.at[d], col_rs.at[d], (gx, bench + mate(d), gz)
        )

    def col_recv(d):
        s = mate_from(d)
        return remote(cols_v.at[s], cols_v.at[s], col_ss.at[d], col_rs.at[d], (gx, bench + s, gz))

    def vp_send(d):
        t = mate(d)
        return remote(
            v_h.at[:, :, pl.ds(pl.multiple_of(t * part, L), part)], vparts.at[seat],
            vp_ss.at[d], vp_rs.at[d], (gx, bench + t, gz),
        )

    def vp_recv(d):
        s = mate_from(d)
        return remote(vparts.at[s], vparts.at[s], vp_ss.at[d], vp_rs.at[d], (gx, bench + s, gz))

    def each(n, f):
        def step(d, c):
            f(d)
            return c

        lax.fori_loop(1, n, step, 0)

    each(team, lambda d: col_send(d).start())

    fields = (u1, u2, u3)

    def vol_x(slot, act):
        for side, have, dx in sides:

            @pl.when(have)
            def _(side=side, dx=dx):
                act(
                    remote(
                        vxs.at[slot, side], vxr.at[slot, 1 - side],
                        vx_ss.at[slot, side], vx_rs.at[slot, 1 - side], (gx + dx, gy, gz),
                    ),
                    0,
                )

    def vol_x_recv(slot):
        for side, have, dx in sides:

            @pl.when(have)
            def _(side=side, dx=dx):
                halo = vxr.at[slot, side]
                remote(
                    halo, halo, vx_ss.at[slot, side], vx_rs.at[slot, side], (gx + dx, gy, gz)
                ).wait_recv()
                value = vxr[slot, side].astype(F32)
                rim = side * (CX + 1)
                edge = side * (CX - 1)
                if slot == 0:
                    u1[rim] = value
                elif slot == 1:
                    u1[rim] = u1[rim] + value
                    u2[edge + 1] = u2[edge + 1] + rinv[edge] * value
                elif slot == 2:
                    u2[rim] = value + rinv[edge] * vxs[1, side].astype(F32)
                else:
                    u3[rim] = u1[rim] + value

    def vol_send(n, act):
        for side, have, dy in sides_y:

            @pl.when(have)
            def _(side=side, dy=dy):
                act(
                    remote(
                        vys.at[n, side], vyr.at[n, 1 - side],
                        v_ss.at[n, 2 + side], v_rs.at[n, 3 - side], (gx, gy + dy, gz),
                    ),
                    0,
                )

        act(remote(vzs.at[n], vzr.at[n], v_ss.at[n, 4], v_rs.at[n, 4], (gx, gy, other)), 0)

    def vol_recv(n):
        for side, have, dy in sides_y:

            @pl.when(have)
            def _(side=side, dy=dy):
                halo = vyr.at[n, side]
                remote(
                    halo, halo, v_ss.at[n, 2 + side], v_rs.at[n, 2 + side], (gx, gy + dy, gz)
                ).wait_recv()

        remote(vzr.at[n], vzr.at[n], v_ss.at[n, 4], v_rs.at[n, 4], (gx, gy, other)).wait_recv()

    vol_x(0, start)
    vol_send(0, start)

    def tables(table, slot):
        spot = iota((part, total_y), 0) + seat * part
        col = iota((part, total_y), 1)
        cell = jnp.zeros((part, total_y), I32)
        for x in range(CX):
            cell = jnp.where(table[x] == spot, col + x * total_y, cell)
        cell = jnp.sum(cell.astype(F32), axis=1, keepdims=True).astype(I32)
        x = lax.div(cell, total_y)
        y = cell - x * total_y
        y8 = lax.div(y, 8)
        pick[slot] = (iota((part, 16 * n_gy), 1) == y8 * 8 + x).astype(BF16)
        mask[slot] = (lax.div(iota((part, 256), 1), E) == y - y8 * 8).astype(BF16)

    tables(ft, 0)
    spots = iota((tile, L), 0)
    for j in range(n_gy):
        line = jnp.concatenate([ft[x][:, YC * j : YC * (j + 1)] for x in range(CX)], axis=1)
        onehot[:, L * j : L * (j + 1)] = (spots == line).astype(F32).astype(BF16)

    narrow_recv()
    s0, r0, a1, a0 = planes[0], planes[1], planes[2], planes[3]
    s1, r1, a2 = planes[4], planes[5], planes[6]
    lo, hi = yr[0], yr[1]

    def bc(v, n=W):
        return jnp.broadcast_to(v, (CX, n))

    def left(v):
        return pltpu.roll(v, E, 1)

    def right(v):
        return pltpu.roll(v, L - E, 1)

    cor = [[cr[0], cr[1]], [cr[2], cr[3]]]
    edge_u1 = []
    edge_u2 = []
    edge_b1 = []
    for side in range(2):
        hs, hr, h1, h2 = (bc(xr[side, n : n + 1, :]) for n in range(4))
        hu = hs * hr
        at = bc(a0[(CX - 1) * side : (CX - 1) * side + 1, :])
        beside = along_y(hu, left(bc(cor[side][0], L)), right(bc(cor[side][1], L)))
        edge_u1.append(hu)
        edge_b1.append(h1)
        edge_u2.append((hs + h2 + at + h1 + beside) * hr)
    lu2 = lo[0] + left(lo[3]) + right(a0[:, :L]) + lo[2]
    lu2 = (lu2 + along_x(lo[3], bc(cor[0][0], L), bc(cor[1][0], L))) * lo[1]
    hu2 = hi[0] + right(hi[3]) + left(a0[:, W - L :]) + hi[2]
    hu2 = (hu2 + along_x(hi[3], bc(cor[0][1], L), bc(cor[1][1], L))) * hi[1]
    b0 = (s0 + a1 + along_x(a0, edge_u1[0], edge_u1[1]) + along_y(a0, left(lo[3]), right(hi[3]))) * r0
    b1 = (
        s1 + a0 + a2 + along_x(a1, edge_b1[0], edge_b1[1]) + along_y(a1, left(lo[2]), right(hi[2]))
    ) * r1
    face = (s0 + b1 + along_x(b0, edge_u2[0], edge_u2[1]) + along_y(b0, left(lu2), right(hu2))) * r0
    faces[zh, gy] = jnp.concatenate([face[:, : W // 2], face[:, W // 2 :]], axis=0).astype(BF16)

    def ring_d(k):
        half = lax.div(k, 2)
        return n_gy + half * (1 - 2 * lax.rem(k, 2))

    def f_send(k):
        d = ring_d(k)
        bz, by = ring_pos(d)
        return remote(
            faces.at[zh, gy], faces.at[zh, gy], f_ss.at[d], f_rs.at[d], (2 * q + bz, by, gz)
        )

    def f_recv(k):
        d = ring_d(k)
        bz, by = ring_pos(ring - d)
        return remote(
            faces.at[bz, by], faces.at[bz, by], f_ss.at[d], f_rs.at[d], (2 * q + bz, by, gz)
        )

    each(ring, lambda k: f_send(k).start())

    vol_x(1, start)
    each(team, lambda d: vp_send(d).start())

    remote(ft, ftr, ft_sem.at[0], ft_sem.at[1], (anti, gy, gz)).wait_recv()
    tables(ftr, 1)
    u_load.wait()
    flat = far * rank
    u_v_all = u_v[...]
    u_p[:flat, :] = dot_nn(u_v_all, onehot[...]).astype(BF16)
    u_p[flat:, :] = jnp.zeros((L - flat, tile), BF16)
    near_load.wait()
    chunk = min(256, tile)
    for n in range(tile // chunk):
        near_p[n * chunk : (n + 1) * chunk, :] = dot_tn(
            near_v[:, n * chunk : (n + 1) * chunk], onehot[...]
        ).astype(BF16)

    rows32 = iota((DZ, W), 0)
    lanes128 = iota((DZ, L), 1)

    def sweep(n, store):
        u = fields[n]

        def step(k, c):
            for j in range(4):
                x = 4 * k + j
                cell = u[x + 1]
                zrow = vzr[n, x]
                up = jnp.where(rows32 == DZ - 1, jnp.where(gz == 0, zrow, 0.0), pltpu.roll(cell, DZ - 1, 0))
                down = jnp.where(rows32 == 0, jnp.where(gz == 0, 0.0, zrow), pltpu.roll(cell, 1, 0))
                low = pltpu.roll(vyr[n, 0, k], (L - E * j) % L, 1)
                high = pltpu.roll(vyr[n, 1, k], (L - E - E * j) % L, 1)
                total = src[x] + u[x] + u[x + 2] + up + down + along_y(cell, low, high)
                store(x, total)
            return c

        lax.fori_loop(0, CX // 4, step, 0)

    def keep(u):
        def store(x, total):
            u[x + 1] = total * rinv[x]

        return store

    each(team, lambda d: col_recv(d).wait_recv())
    to_smem = pltpu.make_async_copy(cols_v, cols_s, smem_sem)
    to_smem.start()
    to_smem.wait()

    each(ring, lambda k: f_recv(k).wait_recv())

    fold = (lax.rem(iota((E, 256), 1), E) == iota((E, 256), 0)).astype(BF16)
    for slot, (half, block) in enumerate(((zh, gx), (1 - zh, anti))):
        flat_faces = faces[half].reshape(16 * n_gy, 256)
        picked = dot_nn(pick[slot], flat_faces).astype(BF16) * mask[slot]
        gath[gz * n_gx + block] = dot_nt(fold, picked).astype(BF16)

    def mine(qq, side):
        return gath.at[pl.ds(side * n_gx + 2 * qq, 2)]

    def g_send(d):
        t = lax.rem(q + d, nq)
        return remote(mine(q, gz), mine(q, gz), g_ss.at[d], g_rs.at[d], (2 * t + zh, gy, gz))

    def g_recv(d):
        s = lax.rem(q + nq - d, nq)
        return remote(mine(s, gz), mine(s, gz), g_ss.at[d], g_rs.at[d], (2 * s + zh, gy, gz))

    def k_send(d):
        s = lax.rem(q + nq - d, nq)
        return remote(mine(s, gz), mine(s, gz), k_ss.at[d], k_rs.at[d], (gx, gy, other))

    def k_recv(d):
        s = lax.rem(q + nq - d, nq)
        return remote(mine(s, other), mine(s, other), k_ss.at[d], k_rs.at[d], (gx, gy, other))

    each(nq, lambda d: g_send(d).start())
    k_send(0).start()

    vol_x_recv(0)
    vol_recv(0)
    sweep(0, keep(u2))
    pack_x(2)
    vol_x(2, start)

    vol_x_recv(1)
    pack(u2, 1)
    vol_send(1, start)

    v_load.wait()
    each(team, lambda d: vp_recv(d).wait_recv())
    group = lax.div(iota((flat, part), 0), rank)

    def blocks(j, c):
        parts = vparts[j].reshape(flat, part)
        for k in range(far):
            vblk[j, :flat, k * part : (k + 1) * part] = jnp.where(group == k, parts, jnp.zeros_like(parts))
        if flat < L:
            vblk[j, flat:, :] = jnp.zeros((L - flat, far * part), BF16)
        return c

    lax.fori_loop(0, team, blocks, 0)

    def forward(d):
        g_recv(d).wait_recv()
        k_send(d).start()

    each(nq, forward)
    k_recv(0).wait_recv()
    each(nq, lambda d: k_recv(d).wait_recv())

    def w_send(d):
        t = mate(d)
        return remote(ws.at[t], wr.at[seat], w_ss.at[d], w_rs.at[d], (gx, bench + t, gz))

    def w_recv(d):
        s = mate_from(d)
        return remote(wr.at[s], wr.at[s], w_ss.at[d], w_rs.at[d], (gx, bench + s, gz))

    def n_send(d):
        t = mate(d)
        return remote(ns.at[t], nr.at[seat], n_ss.at[d], n_rs.at[d], (gx, bench + t, gz))

    def n_recv(d):
        s = mate_from(d)
        return remote(nr.at[s], nr.at[s], n_ss.at[d], n_rs.at[d], (gx, bench + s, gz))

    def column(j, k):
        c = cols_s[j, 0, k]
        return gath[lax.rem(c, 2) * n_gx + lax.div(c, 2)]

    def partial_weights(t):
        for k in range(far):
            tsel[:, k * part : (k + 1) * part] = column(t, k + 1)
        return dot_nt(tsel[...], vblk[t])

    def near_out(d):
        t = mate(d)
        ns[t] = column(t, 0)
        n_send(d).start()

    each(team, near_out)
    nr[seat] = column(seat, 0)

    def weights_out(d):
        t = mate(d)
        ws[t] = partial_weights(t)
        w_send(d).start()

    each(team, weights_out)
    wr[seat] = partial_weights(seat)

    vol_x_recv(2)
    vol_recv(1)
    sweep(1, keep(u3))
    pack_x(3)
    vol_x(3, start)
    pack(u3, 2)
    vol_send(2, start)

    each(team, lambda d: n_recv(d).wait_recv())
    near_t = jnp.concatenate([nr[j] for j in range(team)], axis=1)
    acc = dot_nn(near_t, near_p[...])
    each(team, lambda d: w_recv(d).wait_recv())
    weights = wr[0]
    for j in range(1, team):
        weights = weights + wr[j]
    acc = acc + dot_nn(weights.astype(BF16), u_p[...])
    for j in range(n_gy):
        rs[j] = acc[:, j * L : (j + 1) * L]
        rsb[j] = acc[:, j * L : (j + 1) * L].astype(BF16)

    def r_send(d):
        t = mate(d)
        return remote(rs.at[bench + t], rr.at[seat], r_ss.at[d], r_rs.at[d], (gx, bench + t, gz))

    def r_recv(d):
        s = mate_from(d)
        return remote(rr.at[s], rr.at[s], r_ss.at[d], r_rs.at[d], (gx, bench + s, gz))

    def b_send(k):
        step = team * (lax.div(k, team) + 1)
        t = lax.rem(bench + step, n_gy) + lax.rem(k, team)
        return remote(
            rsb.at[t], rrb.at[step - team + seat], b_ss.at[k], b_rs.at[step - team + seat], (gx, t, gz)
        )

    def b_recv(k):
        step = team * (lax.div(k, team) + 1)
        s = lax.rem(bench + n_gy - step, n_gy) + lax.rem(k, team)
        return remote(rrb.at[k], rrb.at[k], b_ss.at[k], b_rs.at[k], (gx, s, gz))

    def across(f):
        def step(k, c):
            f(k)
            return c

        lax.fori_loop(0, n_gy - team, step, 0)

    across(lambda k: b_send(k).start())
    each(team, lambda d: r_send(d).start())
    rr[seat] = rs[gy]

    def hold(x, total):
        sol[x] = total

    x_halo(sent)
    c_halo(sent)
    y_halo(sent)
    ft_copy().wait_send()
    each(team, lambda d: col_send(d).wait_send())
    each(team, lambda d: vp_send(d).wait_send())
    each(ring, lambda k: f_send(k).wait_send())
    each(nq, lambda d: g_send(d).wait_send())
    k_send(0).wait_send()
    each(nq, lambda d: k_send(d).wait_send())
    each(team, lambda d: n_send(d).wait_send())
    each(team, lambda d: w_send(d).wait_send())
    for n in range(3):
        vol_send(n, sent)
    for n in range(4):
        vol_x(n, sent)
    vol_x_recv(3)
    vol_recv(2)
    sweep(2, hold)
    each(team, lambda d: r_recv(d).wait_recv())
    across(lambda k: b_recv(k).wait_recv())
    total = rr[0]
    for j in range(1, team):
        total = total + rr[j]
    for j in range(n_gy - team):
        total = total + rrb[j].astype(F32)
    widen = (iota((E, W), 0) == lax.rem(iota((E, W), 1), E)).astype(F32)
    wide = jnp.dot(total.T, widen, precision=HIGHEST, preferred_element_type=F32)
    keep_cell = lax.rem(iota((L, W), 0), YC) == lax.div(iota((L, W), 1), E)
    value = jnp.sum(jnp.where(keep_cell, wide, 0.0).reshape(CX, YC, W), axis=1)
    face_z = (DZ - 1) * gz
    for x in range(CX):
        line = value[x : x + 1, :]
        flux[x] = line
        sol[x] = (sol[x] + jnp.where(rows32 == face_z, line, 0.0)) * rinv[x]

    each(team, lambda d: r_send(d).wait_send())
    across(lambda k: b_send(k).wait_send())


def body(source, coef, face_trace, near_col, far_col, near_tile, far_u, far_v):
    n_gx = lax.axis_size("gx")
    n_gy = lax.axis_size("gy")
    far, rank, tile = far_u.shape[3:]
    total_y = face_trace.shape[2]
    nq, ring, flat = n_gx // 2, 2 * n_gy, far * rank
    team = min(TEAM, n_gy)
    part = tile // team
    cfg = (n_gx, n_gy, far, rank, total_y)
    vmem = pl.BlockSpec(memory_space=pltpu.VMEM)
    anyspace = pl.BlockSpec(memory_space=pl.ANY)
    dma = pltpu.SemaphoreType.DMA
    scratch = [
        pltpu.SMEM((1, 1, 1), I32),
        pltpu.SMEM((1, 1, 1, far), I32),
        pltpu.VMEM((CX, DZ, W), F32),
        pltpu.VMEM((CX, YC, DZ), F32),
        pltpu.VMEM((CX, 1, total_y), I32),
        pltpu.VMEM((CX + 2, DZ, W), F32),
        pltpu.VMEM((CX + 2, DZ, W), F32),
        pltpu.VMEM((CX + 2, DZ, W), F32),
        pltpu.VMEM((CX, DZ, W), F32),
        pltpu.VMEM((7, CX, W), F32),
        pltpu.VMEM((2, 4, W), F32),
        pltpu.VMEM((2, 4, W), F32),
        pltpu.VMEM((2, 4, CX, L), F32),
        pltpu.VMEM((2, 4, CX, L), F32),
        pltpu.VMEM((4, 1, L), F32),
        pltpu.VMEM((4, 1, L), F32),
        pltpu.VMEM((4, 2, DZ, W), BF16),
        pltpu.VMEM((4, 2, DZ, W), BF16),
        pltpu.VMEM((3, 2, CX // 4, DZ, L), F32),
        pltpu.VMEM((3, 2, CX // 4, DZ, L), F32),
        pltpu.VMEM((3, CX, 1, W), F32),
        pltpu.VMEM((3, CX, 1, W), F32),
        pltpu.VMEM((CX, 1, total_y), I32),
        pltpu.VMEM((team, 8, L), I32),
        pltpu.SMEM((team, 8, L), I32),
        pltpu.VMEM((2, part, 16 * n_gy), BF16),
        pltpu.VMEM((2, part, 256), BF16),
        pltpu.VMEM((2, n_gy, 16, 256), BF16),
        pltpu.VMEM((2 * n_gx, E, part), BF16),
        pltpu.VMEM((tile, tile), BF16),
        pltpu.VMEM((tile, tile), BF16),
        pltpu.VMEM((tile, tile), BF16),
        pltpu.VMEM((flat, tile), BF16),
        pltpu.VMEM((L, tile), BF16),
        pltpu.VMEM((team, far, rank, part), BF16),
        pltpu.VMEM((team, L, far * part), BF16),
        pltpu.VMEM((E, far * part), BF16),
        pltpu.VMEM((team, E, part), BF16),
        pltpu.VMEM((team, E, part), BF16),
        pltpu.VMEM((team, E, L), F32),
        pltpu.VMEM((team, E, L), F32),
        pltpu.VMEM((n_gy, E, L), F32),
        pltpu.VMEM((team, E, L), F32),
        pltpu.VMEM((n_gy, E, L), BF16),
        pltpu.VMEM((n_gy, E, L), BF16),
        dma((3,)),
        dma((5,)),
        dma((4,)), dma((4,)),
        dma((4,)), dma((4,)),
        dma((3, 5)), dma((3, 5)),
        dma((4, 2)), dma((4, 2)),
        dma((2,)),
        dma((n_gy,)), dma((n_gy,)),
        dma,
        dma((ring,)), dma((ring,)),
        dma((nq,)), dma((nq,)),
        dma((nq,)), dma((nq,)),
        dma((n_gy,)), dma((n_gy,)),
        dma((n_gy,)), dma((n_gy,)),
        dma((n_gy,)), dma((n_gy,)),
        dma((n_gy,)), dma((n_gy,)),
        dma((n_gy,)), dma((n_gy,)),
    ]
    return pl.pallas_call(
        functools.partial(kernel, cfg),
        out_shape=(
            jax.ShapeDtypeStruct(source.shape, F32),
            jax.ShapeDtypeStruct((CX, 1, W), F32),
        ),
        in_specs=[anyspace] * 8,
        out_specs=(vmem, vmem),
        scratch_shapes=scratch,
        compiler_params=pltpu.CompilerParams(
            collective_id=0, has_side_effects=True, vmem_limit_bytes=60 * 1024 * 1024
        ),
        name="coupled_step",
    )(
        near_col,
        far_col,
        source,
        coef.swapaxes(1, 2),
        face_trace,
        near_tile.reshape(tile, tile),
        far_u.reshape(flat, tile),
        far_v.reshape(far, rank, tile),
    )


def solution(mesh):
    return jax.shard_map(
        body,
        mesh=mesh,
        in_specs=(
            P("gx", "gz", "gy"),
            P("gx", "gz", "gy"),
            P("gx", "gz", None),
            P("gx", "gz", "gy"),
            P("gx", "gz", "gy", None),
            P("gx", "gz", "gy", None, None),
            P("gx", "gz", "gy", None, None, None),
            P("gx", "gz", "gy", None, None, None),
        ),
        out_specs=(P("gx", "gz", "gy"), P("gx", "gz", "gy")),
        check_vma=False,
    )
```
